1024 devices in a mesh: pole: 8 (over x, core), grid: 128 (over z, y).
Axes of the slice: x: 4, y: 8, z: 16, core: 2. Of those that a mesh axis runs over, the one named last changes fastest.
Arguments:
- trailing: bfloat16 [8, 2, 4096, 4096], P('pole', None, 'grid'), may hold values from -4.5 to 4.5, as said below
- panel: bfloat16 [8, 2, 4096, 256], P('pole', None, 'grid'), may hold values from -0.0625 to 0.0625
- diag_inverse: bfloat16 [8, 2, 256, 256], P('pole', None, 'grid'), may hold values from -6 to 6
- pole_weights: float32 [8, 2], P('pole'), may hold values from -2 to 2
- owner_map: int32 [4096, 1], P('grid'), may hold values from 0 to 7; in each aligned block of 32 rows (0 to 31, 32 to 63, ...) at most 8 rows name the same one
- ham_slab: bfloat16 [256, 4096], replicated, may hold values from -0.375 to 0.375
Outputs:
- density_diag: float32 [256, 256], P('grid')
- patch_energy: bfloat16 [8192, 4096], P(('pole', 'grid'))
The draws below stay inside these ranges and needn't reach their ends.
Inputs may be any that keep to these rules, and one draw needn't show every extreme that they name: trailing is symmetric in its last two dimensions: trailing[p, c, i, j] = trailing[p, c, j, i]. `owner_map`: in each aligned block of 32 rows (the rows of one index of grid) at most 8 rows name the same owner, and some block reaches 8.
All inputs are finite; a program needn't handle non-finite values.
Results may differ from the reference program's by a relative error of at most 0.011.
Values may be sent and summed in bfloat16 or wider, within the bound.
No kernel may reach another device: no remote copies, remote signals or barrier semaphores. Data moves between devices by JAX's collectives and lax.ppermute only.
A program may use at most 32 MiB of HBM per device.

```python
import math
import jax
import jax.numpy as jnp
import numpy as np
from jax import lax

M = 4096
W = 256
POLES = 8
RD = 32
CAP = 8
SLOTS = 8192
N_POLE = 8
N_GRID = 128


def draw_trailing(key, part):
    base = jax.random.normal(key, (POLES, 2, M, M), jnp.float32)
    sym = (base + jnp.swapaxes(base, 2, 3)) * math.sqrt(0.5)
    return jnp.clip(sym, -4.5, 4.5).astype(jnp.bfloat16)


def shard_levels(stream_key, extent, cuts, smallest, top_value):
    def one(dim, shards_of):
        heights = jax.random.uniform(jax.random.fold_in(jax.random.fold_in(stream_key, 6), dim), (shards_of,), jnp.float32, smallest / len(cuts), top_value / len(cuts))
        return jnp.repeat(jnp.exp(heights), extent[dim] // shards_of).reshape((-1,) + (1,) * (len(extent) - dim - 1))

    level = one(*cuts[0])
    for cut in cuts[1:]:
        level = level * one(*cut)
    return level


def assign_block(stream_key, own, number, rows, count, top, limit, slope):
    sequence = jax.random.permutation(stream_key, count)
    packed, ordinary = portions_of(count, rows * top, limit, slope, True), portions_of(count, rows * top, limit, slope, False)
    places = jnp.arange(count)

    def named(tallies, offset_by):
        used = int((tallies > 0).sum())
        fixed = max(1, used // 4)
        passed = fixed + (places - fixed + offset_by * (used - fixed)) % max(1, count - fixed)
        return jnp.zeros((count,), jnp.int32).at[sequence[jnp.where(places < fixed, places, passed)]].set(jnp.asarray(tallies, jnp.int32))

    tallies = jnp.where(number % 4 == 0, named(packed, number // 4), named(ordinary, number - number // 4 - 1))
    mixed = jax.random.permutation(jax.random.fold_in(own, 3), count)
    giver, taker = mixed[0:count // 2 * 2:2], mixed[1:count // 2 * 2:2]
    room = jnp.minimum(tallies[giver] - 1, limit - tallies[taker]) // 2
    room = jnp.where((giver == sequence[0]) | (taker == sequence[0]) | (tallies[taker] == 0), 0, jnp.maximum(room, 0))
    passed = jax.random.randint(jax.random.fold_in(own, 4), (count // 2,), 0, 1 << 20) % (room + 1)
    tallies = tallies.at[giver].add(-passed).at[taker].add(passed)
    members = jnp.searchsorted(jnp.cumsum(tallies), jnp.arange(rows * top), side="right").astype(jnp.int32)
    grid = members.reshape(top, rows).T
    grid = grid[jax.random.permutation(jax.random.fold_in(own, 1), rows)]
    offset_by = jax.random.randint(jax.random.fold_in(own, 2), (rows, 1), 0, top)
    return jnp.take_along_axis(grid, (jnp.arange(top)[None, :] + offset_by) % top, axis=1)


def portions_of(amount, total, reach, skew, full):
    weights = [(1 << 20) // math.isqrt(grade ** skew) + 1 for grade in range(1, amount + 1)]
    largest = reach if full else min(reach, max(-(-total // amount), total * weights[0] // sum(weights)))
    least = 1 if total - largest >= amount - 1 else 0
    counts, surplus = [largest] + [least] * (amount - 1), total - largest - least * (amount - 1)
    while surplus > 0:
        candidates = [i for i in range(1, amount) if counts[i] < largest] or [i for i in range(1, amount) if counts[i] < reach]
        whole, remaining = sum([weights[i] for i in candidates]), surplus
        for i in candidates:
            more = min(reach - counts[i], max(1, remaining * weights[i] // whole), surplus)
            counts[i] = counts[i] + more
            surplus = surplus - more
    return np.array(counts)


def centred(own_key, dims, deviation, limit, pieces=(), kind=jnp.bfloat16):
    factor_of = shard_levels(own_key, dims, pieces, -0.22, 0.18) if pieces else 1.0
    drawn = jax.random.normal(own_key, dims, jnp.float32) * deviation * factor_of
    return jnp.minimum(jnp.maximum(drawn, -limit), limit).astype(kind)


def setup_inputs(seed: int = 0) -> dict:
    seeds = jax.random.split(jax.random.key(seed), 7)
    trailing = draw_trailing(jax.random.fold_in(seeds[6], 71), 0)
    panel = centred(seeds[1], (POLES, 2, M, W), (2 * M) ** -0.5, 0.0625, ((0, 8), (2, 128)))
    diag_inverse = centred(seeds[2], (POLES, 2, W, W), 1.0, 6.0, ((0, 8), (2, 128)))
    pole_weights = centred(seeds[3], (POLES, 2), POLES ** -0.5, 2.0, ((0, 8),), jnp.float32)
    owner_map_keys = jax.random.split(jax.random.fold_in(seeds[4], 1), M // RD)
    owner_map_turns = jax.random.permutation(jax.random.fold_in(seeds[4], 3), M // RD)
    owner_map = jax.vmap(lambda own, number: assign_block(jax.random.fold_in(seeds[4], 2), own, number, RD, N_POLE, 1, CAP, 2))(owner_map_keys, owner_map_turns).reshape((M, 1))
    ham_slab = centred(seeds[5], (W, M), W ** -0.5, 0.375)
    return {"trailing": trailing, "panel": panel, "diag_inverse": diag_inverse, "pole_weights": pole_weights, "owner_map": owner_map, "ham_slab": ham_slab}


def batched(form, left, right):
    return jnp.einsum(form, left.astype(jnp.float32), right.astype(jnp.float32))


def reference(trailing, panel, diag_inverse, pole_weights, owner_map, ham_slab):
    grid_real = trailing[:, 0]
    grid_imag = trailing[:, 1]
    low_real = panel[:, 0]
    low_imag = panel[:, 1]
    form = "pmn,pnw->pmw"
    cross_real = -(batched(form, grid_real, low_real) - batched(form, grid_imag, low_imag))
    cross_imag = -(batched(form, grid_real, low_imag) + batched(form, grid_imag, low_real))
    cross_real = cross_real.astype(jnp.bfloat16).astype(jnp.float32)
    cross_imag = cross_imag.astype(jnp.bfloat16).astype(jnp.float32)
    weight_real = pole_weights[:, 0][:, None, None]
    weight_imag = pole_weights[:, 1][:, None, None]
    density_rows = jnp.sum(weight_real * cross_imag + weight_imag * cross_real, axis=0)
    density_half = density_rows.astype(jnp.bfloat16)
    tform = "pmw,pmv->pwv"
    quad_real = batched(tform, low_real, cross_real) - batched(tform, low_imag, cross_imag)
    quad_imag = batched(tform, low_real, cross_imag) + batched(tform, low_imag, cross_real)
    inverse_real = diag_inverse[:, 0].astype(jnp.float32) - quad_real
    inverse_imag = diag_inverse[:, 1].astype(jnp.float32) - quad_imag
    density_diag = jnp.sum(weight_real * inverse_imag + weight_imag * inverse_real, axis=0)
    owners = owner_map[:, 0].astype(jnp.int32)
    positions = lax.broadcasted_iota(jnp.int32, (M,), 0)
    shard = positions // RD
    keyed = shard * N_POLE + owners
    same = keyed[:, None] == keyed[None, :]
    earlier = positions[None, :] < positions[:, None]
    rank = jnp.sum((same & earlier).astype(jnp.int32), axis=1)
    slot = owners * (N_GRID * CAP) + shard * CAP + rank
    patch = jnp.zeros((SLOTS, W), jnp.float32).at[slot].set(density_half.astype(jnp.float32))
    patch = patch.astype(jnp.bfloat16)
    patch_energy = jnp.dot(patch, ham_slab, preferred_element_type=jnp.float32).astype(jnp.bfloat16)
    return (density_diag, patch_energy)
```

```python
import jax
import jax.numpy as jnp
from jax import lax
from jax.experimental import pallas as pl
from jax.experimental.pallas import tpu as pltpu
from jax.sharding import Mesh, PartitionSpec as P

NX, NC, NZ, NY = 4, 2, 16, 8
NP = NX * NC
RD = 32
W = 256
ZR = NY * RD
YC = NZ * RD
CAP = 8
F32 = jnp.float32
BF16 = jnp.bfloat16
VM = pl.BlockSpec(memory_space=pltpu.VMEM)
SM = pl.BlockSpec(memory_space=pltpu.SMEM)


def kernel_call(body, outs, specs, name, flops=0, moved=0):
    shapes = tuple(jax.ShapeDtypeStruct(s, d) for s, d in outs)
    return pl.pallas_call(
        body,
        out_shape=shapes,
        in_specs=specs,
        out_specs=tuple(VM for _ in outs),
        name=name,
        cost_estimate=pl.CostEstimate(flops=flops, bytes_accessed=moved, transcendentals=0),
    )


def pack_kernel(g_ref, l_ref, out_ref, own_ref):
    quarter = lax.broadcasted_iota(jnp.int32, (RD, 128), 1) // 32
    for part in range(2):
        for half in range(2):
            for tile in range(4):
                loaded = [
                    g_ref[0, part, :, (4 * tile + j) * W + half * 128 : (4 * tile + j) * W + half * 128 + 128].astype(F32)
                    for j in range(4)
                ]
                for q in range(4):
                    joined = None
                    for j in range(4):
                        shift = (32 * (j - q)) % 128
                        moved = pltpu.roll(loaded[j], shift, 1) if shift else loaded[j]
                        joined = moved if joined is None else jnp.where(quarter == j, moved, joined)
                    out_ref[4 * half + q, RD * part : RD * part + RD, 128 * tile : 128 * tile + 128] = joined.astype(BF16)
    for part in range(2):
        rows = l_ref[0, part]
        own_ref[:, W * part : W * part + W] = rows
        for y in range(NY):
            out_ref[y, 2 * RD : 3 * RD, W * part : W * part + W] = rows


def cross_kernel(w_ref, b_ref, l_ref, out_ref):
    wr = w_ref[0, 0]
    wi = w_ref[0, 1]
    columns = l_ref[...].reshape(YC, 2 * W)
    first = jnp.dot(b_ref[:, 0:RD, :].reshape(ZR, YC), columns, preferred_element_type=F32)
    second = jnp.dot(b_ref[:, RD : 2 * RD, :].reshape(ZR, YC), columns, preferred_element_type=F32)
    real = first[:, :W] - second[:, W:]
    imag = first[:, W:] + second[:, :W]
    even = wr * imag + wi * real
    odd = wr * real - wi * imag
    rows = b_ref[:, 2 * RD : 3 * RD, :].reshape(ZR, 2 * W)
    over_rows = (((0,), (0,)), ((), ()))
    quad = lax.dot_general(rows[:, :W], even.astype(BF16), over_rows, preferred_element_type=F32)
    quad = quad + lax.dot_general(rows[:, W:], odd.astype(BF16), over_rows, preferred_element_type=F32)
    to = lax.broadcasted_iota(jnp.int32, (W, W), 0)
    source = (to % 32) // 2 * 16 + to // 32 * 2 + to % 2
    order = (lax.broadcasted_iota(jnp.int32, (W, W), 1) == source).astype(F32).astype(BF16)
    quad = jnp.dot(order, quad.astype(BF16), preferred_element_type=F32).astype(BF16)
    density = (-even).astype(BF16)
    for y in range(NY):
        out_ref[y, :, 0:W] = density[RD * y : RD * y + RD]
        out_ref[y, :, W : 2 * W] = quad[RD * y : RD * y + RD]


def slot_kernel(o_ref, p_ref, slots_ref, quad_ref):
    total = jnp.sum(p_ref[...].astype(F32), axis=0)
    owner = jnp.broadcast_to(o_ref[...], (RD, RD))
    row = lax.broadcasted_iota(jnp.int32, (RD, RD), 0)
    column = lax.broadcasted_iota(jnp.int32, (RD, RD), 1)
    owner_down = jnp.sum(jnp.where(row == column, owner, 0), axis=1, keepdims=True)
    earlier = (owner_down == owner) & (row < column)
    rank = jnp.sum(earlier.astype(jnp.int32), axis=0, keepdims=True)
    slot = o_ref[...] * CAP + rank
    place = (lax.broadcasted_iota(jnp.int32, (NP * CAP, RD), 0) == slot).astype(F32)
    slots = jnp.dot(place, total[:, :W], precision=lax.Precision.HIGHEST, preferred_element_type=F32)
    for k in range(NP):
        slots_ref[k] = slots[CAP * k : CAP * k + CAP]
    for z in range(NZ):
        quad_ref[z] = total[2 * z : 2 * z + 2, W : 2 * W]


def join_kernel(w_ref, q_ref, d_ref, s_ref, out_ref):
    quad = jnp.sum(q_ref[...], axis=0)
    quad = quad + w_ref[0, 0] * d_ref[0, 1].astype(F32) + w_ref[0, 1] * d_ref[0, 0].astype(F32)
    zero = jnp.zeros((CAP - 2, W), F32)
    for k in range(NP):
        out_ref[k, 0:CAP] = s_ref[k]
        out_ref[k, CAP : CAP + 2] = quad
        out_ref[k, CAP + 2 :] = zero


def energy_kernel(p_ref, h_ref, diag_ref, energy_ref):
    total = jnp.sum(p_ref[...], axis=0)
    half = total[0:CAP].astype(BF16)
    energy_ref[...] = jnp.dot(half, h_ref[...], preferred_element_type=F32).astype(BF16)
    diag_ref[...] = total[CAP : CAP + 2]


def per_device(trailing, panel, diag_inverse, pole_weights, owner_map, ham_slab):
    packed, own = kernel_call(
        pack_kernel, [((NY, 3 * RD, YC), BF16), ((RD, 2 * W), BF16)], [VM, VM], "pack", moved=1 << 20
    )(trailing, panel)
    columns = lax.all_gather(own, "z")
    block = lax.all_to_all(packed, "y", 0, 0)
    (partial,) = kernel_call(
        cross_kernel, [((NY, RD, 2 * W), BF16)], [SM, VM, VM], "cross", flops=1 << 29, moved=1 << 20
    )(pole_weights, block, columns)
    partial = lax.all_to_all(partial, "y", 0, 0)
    slots, quad = kernel_call(
        slot_kernel, [((NP, CAP, W), F32), ((NZ, 2, W), F32)], [VM, VM], "slot", moved=1 << 18
    )(owner_map.reshape(1, RD), partial)
    quad = lax.all_to_all(quad, "z", 0, 0)
    (joined,) = kernel_call(
        join_kernel, [((NP, 2 * CAP, W), F32)], [SM, VM, VM, VM], "join", moved=1 << 18
    )(pole_weights, quad, diag_inverse, slots)
    joined = lax.all_to_all(joined, ("x", "c"), 0, 0)
    density_diag, patch_energy = kernel_call(
        energy_kernel, [((2, W), F32), ((CAP, NZ * NY * RD), BF16)], [VM, VM], "energy", flops=1 << 24, moved=1 << 21
    )(joined, ham_slab)
    return (density_diag, patch_energy)


def solution(mesh):
    fine = Mesh(mesh.devices.reshape(NX, NC, NZ, NY), ("x", "c", "z", "y"))
    pole, grid = ("x", "c"), ("z", "y")
    by_row = P(pole, None, grid, None)
    return jax.shard_map(
        per_device,
        mesh=fine,
        in_specs=(by_row, by_row, by_row, P(pole, None), P(grid, None), P()),
        out_specs=(P(grid, None), P(("x", "c", "z", "y"), None)),
        check_vma=False,
    )
```

```python
import jax
import jax.numpy as jnp
from jax import lax
from jax.experimental import pallas as pl
from jax.experimental.pallas import tpu as pltpu
from jax.sharding import Mesh, PartitionSpec as P

NX, NC, NZ, NY = 4, 2, 16, 8
NP = NX * NC
RD = 32
W = 256
ZR = NY * RD
YC = NZ * RD
CAP = 8
TAIL = 16
F32 = jnp.float32
BF16 = jnp.bfloat16
VM = pl.BlockSpec(memory_space=pltpu.VMEM)
SM = pl.BlockSpec(memory_space=pltpu.SMEM)


def kernel_call(body, outs, specs, flops=0, moved=0):
    shapes = tuple(jax.ShapeDtypeStruct(s, d) for s, d in outs)
    return pl.pallas_call(
        body,
        out_shape=shapes,
        in_specs=specs,
        out_specs=tuple(VM for _ in outs),
        cost_estimate=pl.CostEstimate(flops=flops, bytes_accessed=moved, transcendentals=0),
    )


def pack_kernel(o_ref, g_ref, l_ref, out_ref, own_ref):
    owner = jnp.broadcast_to(o_ref[...], (RD, RD))
    row = lax.broadcasted_iota(jnp.int32, (RD, RD), 0)
    column = lax.broadcasted_iota(jnp.int32, (RD, RD), 1)
    owner_down = jnp.sum(jnp.where(row == column, owner, 0), axis=1, keepdims=True)
    earlier = (owner_down == owner) & (row < column)
    rank = jnp.sum(earlier.astype(jnp.int32), axis=0, keepdims=True)
    slot = (o_ref[...] * CAP + rank).astype(F32)
    slot = jnp.broadcast_to(slot, (TAIL, RD)).astype(BF16)
    for y in range(NY):
        out_ref[y, 3 * RD :, :] = jnp.zeros((TAIL, YC), BF16)
        out_ref[y, 3 * RD :, 0:RD] = slot
    quarter = lax.broadcasted_iota(jnp.int32, (RD, 128), 1) // 32
    for part in range(2):
        for half in range(2):
            for tile in range(4):
                loaded = [
                    g_ref[0, part, :, (4 * tile + j) * W + half * 128 : (4 * tile + j) * W + half * 128 + 128].astype(F32)
                    for j in range(4)
                ]
                for q in range(4):
                    joined = None
                    for j in range(4):
                        shift = (32 * (j - q)) % 128
                        moved = pltpu.roll(loaded[j], shift, 1) if shift else loaded[j]
                        joined = moved if joined is None else jnp.where(quarter == j, moved, joined)
                    out_ref[4 * half + q, RD * part : RD * part + RD, 128 * tile : 128 * tile + 128] = joined.astype(BF16)
    for part in range(2):
        rows = l_ref[0, part]
        own_ref[:, W * part : W * part + W] = rows
        for y in range(NY):
            out_ref[y, 2 * RD : 3 * RD, W * part : W * part + W] = rows


def cross_kernel(w_ref, b_ref, l_ref, density_ref, quad_ref):
    wr = w_ref[0, 0]
    wi = w_ref[0, 1]
    columns = l_ref[...].reshape(YC, 2 * W)
    first = jnp.dot(b_ref[:, 0:RD, :].reshape(ZR, YC), columns, preferred_element_type=F32)
    second = jnp.dot(b_ref[:, RD : 2 * RD, :].reshape(ZR, YC), columns, preferred_element_type=F32)
    real = first[:, :W] - second[:, W:]
    imag = first[:, W:] + second[:, :W]
    even = wr * imag + wi * real
    odd = wr * real - wi * imag
    rows = b_ref[:, 2 * RD : 3 * RD, :].reshape(ZR, 2 * W)
    over_rows = (((0,), (0,)), ((), ()))
    quad = lax.dot_general(rows[:, :W], even.astype(BF16), over_rows, preferred_element_type=F32)
    quad = quad + lax.dot_general(rows[:, W:], odd.astype(BF16), over_rows, preferred_element_type=F32)
    quad_ref[...] = quad.astype(BF16).reshape(NZ, W // NZ, W)
    density_ref[...] = (-even).astype(BF16)


def place_kernel(s_ref, density_ref, out_ref):
    index = lax.broadcasted_iota(jnp.int32, (NP * CAP, RD), 0)
    for y in range(NY):
        slot = s_ref[y, 0:1, 0:RD].astype(F32).astype(jnp.int32)
        place = (index == slot).astype(F32).astype(BF16)
        rows = density_ref[RD * y : RD * y + RD, :]
        placed = jnp.dot(place, rows, preferred_element_type=F32).astype(BF16)
        for k in range(NP):
            out_ref[NY * k + y] = placed[CAP * k : CAP * k + CAP]


def join_kernel(w_ref, q_ref, d_ref, p_ref, out_ref):
    quad = jnp.sum(q_ref[...].astype(F32), axis=0)
    diag = w_ref[0, 0] * d_ref[0, 1].astype(F32) + w_ref[0, 1] * d_ref[0, 0].astype(F32)
    here = lax.axis_index("y")
    zero = jnp.zeros((CAP - 4, 128), F32)
    for y in range(NY):
        rows = quad[2 * y : 2 * y + 2] + jnp.where(here == y, diag, 0.0)
        tail = jnp.concatenate([rows[:, :128], rows[:, 128:], zero], axis=0).astype(BF16)
        for k in range(NP):
            out_ref[NY * k + y, :, 0:W] = p_ref[NY * k + y]
            out_ref[NY * k + y, :, W:] = tail


def energy_kernel(p_ref, h_ref, diag_ref, energy_ref):
    total = jnp.sum(p_ref[...].astype(F32), axis=0)
    half = total[:, :W].astype(BF16)
    energy_ref[...] = jnp.dot(half, h_ref[...], preferred_element_type=F32).astype(BF16)
    diag_ref[:, 0:128] = total[0:2, W:]
    diag_ref[:, 128:] = total[2:4, W:]


def per_device(trailing, panel, diag_inverse, pole_weights, owner_map, ham_slab):
    packed, own = kernel_call(
        pack_kernel, [((NY, 3 * RD + TAIL, YC), BF16), ((RD, 2 * W), BF16)], [VM] * 3, moved=1 << 20
    )(owner_map.reshape(1, RD), trailing, panel)
    block = lax.all_to_all(packed, "y", 0, 0)
    columns = lax.all_gather(own, "z")
    density, quad = kernel_call(
        cross_kernel, [((ZR, W), BF16), ((NZ, W // NZ, W), BF16)], [SM, VM, VM], flops=1 << 29, moved=1 << 20
    )(pole_weights, block, columns)
    quad = lax.all_to_all(quad, "z", 0, 0)
    (placed,) = kernel_call(
        place_kernel, [((NP * NY, CAP, W), BF16)], [VM, VM], flops=1 << 23, moved=1 << 18
    )(block[:, 3 * RD :, :128], density)
    (joined,) = kernel_call(
        join_kernel, [((NP * NY, CAP, W + 128), BF16)], [SM, VM, VM, VM], moved=1 << 18
    )(pole_weights, quad, diag_inverse, placed)
    joined = lax.all_to_all(joined, ("x", "c", "y"), 0, 0)
    density_diag, patch_energy = kernel_call(
        energy_kernel, [((2, W), F32), ((CAP, NZ * NY * RD), BF16)], [VM, VM], flops=1 << 24, moved=1 << 21
    )(joined, ham_slab)
    return (density_diag, patch_energy)


def solution(mesh):
    fine = Mesh(mesh.devices.reshape(NX, NC, NZ, NY), ("x", "c", "z", "y"))
    pole, grid = ("x", "c"), ("z", "y")
    by_row = P(pole, None, grid, None)
    return jax.shard_map(
        per_device,
        mesh=fine,
        in_specs=(by_row, by_row, by_row, P(pole, None), P(grid, None), P()),
        out_specs=(P(grid, None), P(("x", "c", "z", "y"), None)),
        check_vma=False,
    )
```

```python
import jax
import jax.numpy as jnp
from jax import lax
from jax.experimental import pallas as pl
from jax.experimental.pallas import tpu as pltpu
from jax.sharding import Mesh, PartitionSpec as P

NX, NC, NZ, NY = 4, 2, 16, 8
NP = NX * NC
RD = 32
W = 256
ZR = NY * RD
YC = NZ * RD
CAP = 8
TAIL = 16
F32 = jnp.float32
BF16 = jnp.bfloat16
VM = pl.BlockSpec(memory_space=pltpu.VMEM)
SM = pl.BlockSpec(memory_space=pltpu.SMEM)


def kernel_call(body, outs, specs, flops=0, moved=0, kept=(True, True)):
    call = pl.pallas_call(
        body,
        out_shape=tuple(pltpu.VMEM(s, d) if k else jax.ShapeDtypeStruct(s, d) for (s, d), k in zip(outs, kept)),
        in_specs=specs,
        out_specs=tuple(VM for _ in outs),
        cost_estimate=pl.CostEstimate(flops=flops, bytes_accessed=moved, transcendentals=0),
    )

    def run(*args):
        return call(
            *(
                pltpu.with_memory_space_constraint(arg, pltpu.VMEM) if spec is VM else arg
                for arg, spec in zip(args, specs, strict=True)
            )
        )

    return run


def pack_kernel(o_ref, g_ref, l_ref, out_ref, own_ref):
    owner = jnp.broadcast_to(o_ref[...], (RD, RD))
    row = lax.broadcasted_iota(jnp.int32, (RD, RD), 0)
    column = lax.broadcasted_iota(jnp.int32, (RD, RD), 1)
    owner_down = jnp.sum(jnp.where(row == column, owner, 0), axis=1, keepdims=True)
    earlier = (owner_down == owner) & (row < column)
    rank = jnp.sum(earlier.astype(jnp.int32), axis=0, keepdims=True)
    slot = (o_ref[...] * CAP + rank).astype(F32)
    slot = jnp.broadcast_to(slot, (TAIL, RD)).astype(BF16)
    for y in range(NY):
        out_ref[y, 3 * RD :, :] = jnp.zeros((TAIL, YC), BF16)
        out_ref[y, 3 * RD :, 0:RD] = slot
    quarter = lax.broadcasted_iota(jnp.int32, (RD, 128), 1) // 32
    for part in range(2):
        for half in range(2):
            for tile in range(4):
                loaded = [
                    g_ref[0, part, :, (4 * tile + j) * W + half * 128 : (4 * tile + j) * W + half * 128 + 128].astype(F32)
                    for j in range(4)
                ]
                for q in range(4):
                    joined = None
                    for j in range(4):
                        shift = (32 * (j - q)) % 128
                        moved = pltpu.roll(loaded[j], shift, 1) if shift else loaded[j]
                        joined = moved if joined is None else jnp.where(quarter == j, moved, joined)
                    out_ref[4 * half + q, RD * part : RD * part + RD, 128 * tile : 128 * tile + 128] = joined.astype(BF16)
    for part in range(2):
        rows = l_ref[0, part]
        own_ref[:, W * part : W * part + W] = rows
        for y in range(NY):
            out_ref[y, 2 * RD : 3 * RD, W * part : W * part + W] = rows


def cross_kernel(w_ref, b_ref, l_ref, density_ref, quad_ref):
    wr = w_ref[0, 0]
    wi = w_ref[0, 1]
    columns = l_ref[...].reshape(YC, 2 * W)
    first = jnp.dot(b_ref[:, 0:RD, :].reshape(ZR, YC), columns, preferred_element_type=F32)
    second = jnp.dot(b_ref[:, RD : 2 * RD, :].reshape(ZR, YC), columns, preferred_element_type=F32)
    real = first[:, :W] - second[:, W:]
    imag = first[:, W:] + second[:, :W]
    even = wr * imag + wi * real
    odd = wr * real - wi * imag
    rows = b_ref[:, 2 * RD : 3 * RD, :].reshape(ZR, 2 * W)
    over_rows = (((0,), (0,)), ((), ()))
    quad = lax.dot_general(rows[:, :W], even.astype(BF16), over_rows, preferred_element_type=F32)
    quad = quad + lax.dot_general(rows[:, W:], odd.astype(BF16), over_rows, preferred_element_type=F32)
    quad_ref[...] = quad.astype(BF16).reshape(NZ, W // NZ, W)
    density_ref[...] = (-even).astype(BF16)


def place_kernel(s_ref, density_ref, out_ref):
    index = lax.broadcasted_iota(jnp.int32, (NP * CAP, RD), 0)
    for y in range(NY):
        slot = s_ref[y, 0:1, 0:RD].astype(F32).astype(jnp.int32)
        place = (index == slot).astype(F32).astype(BF16)
        rows = density_ref[RD * y : RD * y + RD, :]
        placed = jnp.dot(place, rows, preferred_element_type=F32).astype(BF16)
        for k in range(NP):
            out_ref[NY * k + y] = placed[CAP * k : CAP * k + CAP]


def join_kernel(w_ref, q_ref, d_ref, p_ref, out_ref):
    quad = jnp.sum(q_ref[...].astype(F32), axis=0)
    diag = w_ref[0, 0] * d_ref[0, 1].astype(F32) + w_ref[0, 1] * d_ref[0, 0].astype(F32)
    here = lax.axis_index("y")
    zero = jnp.zeros((CAP - 4, 128), F32)
    for y in range(NY):
        rows = quad[2 * y : 2 * y + 2] + jnp.where(here == y, diag, 0.0)
        tail = jnp.concatenate([rows[:, :128], rows[:, 128:], zero], axis=0).astype(BF16)
        for k in range(NP):
            out_ref[NY * k + y, :, 0:W] = p_ref[NY * k + y]
            out_ref[NY * k + y, :, W:] = tail


def total_kernel(p_ref, half_ref, diag_ref):
    total = jnp.sum(p_ref[...].astype(F32), axis=0)
    half_ref[...] = total[:, :W].astype(BF16)
    diag_ref[:, 0:128] = total[0:2, W:]
    diag_ref[:, 128:] = total[2:4, W:]


def per_device(trailing, panel, diag_inverse, pole_weights, owner_map, ham_slab):
    packed, own = kernel_call(
        pack_kernel, [((NY, 3 * RD + TAIL, YC), BF16), ((RD, 2 * W), BF16)], [VM] * 3, moved=1 << 20
    )(owner_map.reshape(1, RD), trailing, panel)
    block = lax.all_to_all(packed, "y", 0, 0)
    columns = lax.all_gather(own, "z")
    density, quad = kernel_call(
        cross_kernel, [((ZR, W), BF16), ((NZ, W // NZ, W), BF16)], [SM, VM, VM], flops=1 << 29, moved=1 << 20
    )(pole_weights, block, columns)
    quad = lax.all_to_all(quad, "z", 0, 0)
    (placed,) = kernel_call(
        place_kernel, [((NP * NY, CAP, W), BF16)], [VM, VM], flops=1 << 23, moved=1 << 18
    )(block[:, 3 * RD :, :128], density)
    (joined,) = kernel_call(
        join_kernel, [((NP * NY, CAP, W + 128), BF16)], [SM, VM, VM, VM], moved=1 << 18
    )(pole_weights, quad, diag_inverse, placed)
    joined = lax.all_to_all(joined, ("x", "c", "y"), 0, 0)
    half, density_diag = kernel_call(
        total_kernel, [((CAP, W), BF16), ((2, W), F32)], [VM], moved=1 << 18, kept=(True, False)
    )(joined)
    patch_energy = jnp.dot(half, ham_slab, preferred_element_type=F32).astype(BF16)
    return (density_diag, patch_energy)


def solution(mesh):
    fine = Mesh(mesh.devices.reshape(NX, NC, NZ, NY), ("x", "c", "z", "y"))
    pole, grid = ("x", "c"), ("z", "y")
    by_row = P(pole, None, grid, None)
    return jax.shard_map(
        per_device,
        mesh=fine,
        in_specs=(by_row, by_row, by_row, P(pole, None), P(grid, None), P()),
        out_specs=(P(grid, None), P(("x", "c", "z", "y"), None)),
        check_vma=False,
    )
```

```python
import jax
import jax.numpy as jnp
from jax import lax
from jax.experimental import pallas as pl
from jax.experimental.pallas import tpu as pltpu
from jax.sharding import Mesh, PartitionSpec as P

NX, NC, NZ, NY = 4, 2, 16, 8
RD = 32
W = 256
ZR = NY * RD
YC = NZ * RD
CAP = 8
TAIL = 16
F32 = jnp.float32
BF16 = jnp.bfloat16
VM = pl.BlockSpec(memory_space=pltpu.VMEM)
SM = pl.BlockSpec(memory_space=pltpu.SMEM)


def kernel_call(body, outs, specs, flops=0, moved=0, kept=(True, True)):
    call = pl.pallas_call(
        body,
        out_shape=tuple(pltpu.VMEM(s, d) if k else jax.ShapeDtypeStruct(s, d) for (s, d), k in zip(outs, kept)),
        in_specs=specs,
        out_specs=tuple(VM for _ in outs),
        cost_estimate=pl.CostEstimate(flops=flops, bytes_accessed=moved, transcendentals=0),
    )

    def run(*args):
        return call(
            *(
                pltpu.with_memory_space_constraint(arg, pltpu.VMEM) if spec is VM else arg
                for arg, spec in zip(args, specs, strict=True)
            )
        )

    return run


def pack_kernel(o_hbm, g_hbm, l_hbm, out_hbm, own_ref, o_ref, g_ref, l_ref, out_ref, in_sem, out_sem):
    owners_in = pltpu.make_async_copy(o_hbm, o_ref, in_sem.at[0])
    rows_in = pltpu.make_async_copy(l_hbm, l_ref, in_sem.at[1])
    wide = NZ * W // 2
    pieces_in = [
        [
            pltpu.make_async_copy(
                g_hbm.at[0, part, :, pl.ds(wide * side, wide)],
                g_ref.at[part, :, pl.ds(wide * side, wide)],
                in_sem.at[2 + 2 * part + side],
            )
            for side in range(2)
        ]
        for part in range(2)
    ]
    pieces_out = [
        pltpu.make_async_copy(
            out_ref.at[:, pl.ds(start, size), :], out_hbm.at[:, pl.ds(start, size), :], out_sem.at[i]
        )
        for i, (start, size) in enumerate(((0, RD), (RD, RD), (2 * RD, RD + TAIL)))
    ]
    for part in range(2):
        for side in range(2):
            pieces_in[part][side].start()
    owners_in.start()
    rows_in.start()
    quarter = lax.broadcasted_iota(jnp.int32, (RD, 128), 1) // 32
    for part in range(2):
        for tile in range(4):
            if tile % 2 == 0:
                pieces_in[part][tile // 2].wait()
            for half in range(2):
                loaded = [
                    g_ref[part, :, (4 * tile + j) * W + half * 128 : (4 * tile + j) * W + half * 128 + 128].astype(F32)
                    for j in range(4)
                ]
                for q in range(4):
                    joined = None
                    for j in range(4):
                        shift = (32 * (j - q)) % 128
                        moved = pltpu.roll(loaded[j], shift, 1) if shift else loaded[j]
                        joined = moved if joined is None else jnp.where(quarter == j, moved, joined)
                    out_ref[4 * half + q, RD * part : RD * part + RD, 128 * tile : 128 * tile + 128] = joined.astype(BF16)
        pieces_out[part].start()
        if part == 0:
            owners_in.wait()
            rows_in.wait()
            owner = jnp.broadcast_to(o_ref[...], (RD, RD))
            row = lax.broadcasted_iota(jnp.int32, (RD, RD), 0)
            column = lax.broadcasted_iota(jnp.int32, (RD, RD), 1)
            owner_down = jnp.sum(jnp.where(row == column, owner, 0), axis=1, keepdims=True)
            earlier = (owner_down == owner) & (row < column)
            rank = jnp.sum(earlier.astype(jnp.int32), axis=0, keepdims=True)
            slot = (o_ref[...] * CAP + rank).astype(F32)
            slot = jnp.broadcast_to(slot, (TAIL, RD)).astype(BF16)
            for y in range(NY):
                out_ref[y, 3 * RD :, :] = jnp.zeros((TAIL, YC), BF16)
                out_ref[y, 3 * RD :, 0:RD] = slot
            for side in range(2):
                rows = l_ref[0, side]
                own_ref[:, W * side : W * side + W] = rows
                for y in range(NY):
                    out_ref[y, 2 * RD : 3 * RD, W * side : W * side + W] = rows
            pieces_out[2].start()
    for piece in pieces_out:
        piece.wait()


def pack(owner_map, trailing, panel):
    packed = (NY, 3 * RD + TAIL, YC)
    anywhere = pl.BlockSpec(memory_space=pl.ANY)
    return pl.pallas_call(
        pack_kernel,
        out_shape=(jax.ShapeDtypeStruct(packed, BF16), pltpu.VMEM((RD, 2 * W), BF16)),
        in_specs=[anywhere] * 3,
        out_specs=(anywhere, VM),
        scratch_shapes=[
            pltpu.VMEM((1, RD), jnp.int32),
            pltpu.VMEM((2, RD, NZ * W), BF16),
            pltpu.VMEM((1, 2, RD, W), BF16),
            pltpu.VMEM(packed, BF16),
            pltpu.SemaphoreType.DMA((6,)),
            pltpu.SemaphoreType.DMA((3,)),
        ],
        name="pack",
        cost_estimate=pl.CostEstimate(flops=0, bytes_accessed=1 << 20, transcendentals=0),
    )(owner_map.reshape(1, RD), trailing, panel)


def cross_kernel(w_ref, b_ref, l_ref, density_ref, quad_ref):
    wr = w_ref[0, 0]
    wi = w_ref[0, 1]
    columns = l_ref[...].reshape(YC, 2 * W)
    first = jnp.dot(b_ref[:, 0:RD, :].reshape(ZR, YC), columns, preferred_element_type=F32)
    second = jnp.dot(b_ref[:, RD : 2 * RD, :].reshape(ZR, YC), columns, preferred_element_type=F32)
    real = first[:, :W] - second[:, W:]
    imag = first[:, W:] + second[:, :W]
    even = wr * imag + wi * real
    odd = wr * real - wi * imag
    rows = b_ref[:, 2 * RD : 3 * RD, :].reshape(ZR, 2 * W)
    over_rows = (((0,), (0,)), ((), ()))
    quad = lax.dot_general(rows[:, :W], even.astype(BF16), over_rows, preferred_element_type=F32)
    quad = quad + lax.dot_general(rows[:, W:], odd.astype(BF16), over_rows, preferred_element_type=F32)
    quad_ref[...] = quad.astype(BF16).reshape(NZ, W // NZ, W)
    density_ref[...] = (-even).astype(BF16)


def place_kernel(s_ref, density_ref, mine_ref, other_ref):
    core = lax.axis_index("c")
    line = lax.broadcasted_iota(jnp.int32, (2 * NX * CAP, RD), 0)
    half = line // (NX * CAP)
    within = line % (NX * CAP)
    side = jnp.where(half == 0, core, 1 - core)
    index = (within // CAP * NC + side) * CAP + within % CAP
    for y in range(NY):
        slot = s_ref[y, 0:1, 0:RD].astype(F32).astype(jnp.int32)
        place = (index == slot).astype(F32).astype(BF16)
        rows = density_ref[RD * y : RD * y + RD, :]
        placed = jnp.dot(place, rows, preferred_element_type=F32).astype(BF16)
        for x in range(NX):
            mine_ref[NY * x + y] = placed[CAP * x : CAP * x + CAP]
            other_ref[NY * x + y] = placed[CAP * (NX + x) : CAP * (NX + x) + CAP]


def join_kernel(w_ref, q_ref, d_ref, p_ref, o_ref, out_ref):
    quad = jnp.sum(q_ref[...].astype(F32), axis=0)
    diag = w_ref[0, 0] * d_ref[0, 1].astype(F32) + w_ref[0, 1] * d_ref[0, 0].astype(F32)
    here = lax.axis_index("y")
    zero = jnp.zeros((CAP - 4, 128), F32)
    out_ref[:, :, 0:W] = (p_ref[...].astype(F32) + o_ref[...].astype(F32)).astype(BF16)
    for y in range(NY):
        rows = quad[2 * y : 2 * y + 2] + jnp.where(here == y, diag, 0.0)
        tail = jnp.concatenate([rows[:, :128], rows[:, 128:], zero], axis=0).astype(BF16)
        for x in range(NX):
            out_ref[NY * x + y, :, W:] = tail


def total_kernel(p_ref, half_ref, diag_ref):
    total = jnp.sum(p_ref[...].astype(F32), axis=0)
    half_ref[...] = total[:, :W].astype(BF16)
    diag_ref[:, 0:128] = total[0:2, W:]
    diag_ref[:, 128:] = total[2:4, W:]


def per_device(trailing, panel, diag_inverse, pole_weights, owner_map, ham_slab):
    packed, own = pack(owner_map, trailing, panel)
    block = lax.all_to_all(packed, "y", 0, 0)
    columns = lax.all_gather(own, "z")
    density, quad = kernel_call(
        cross_kernel, [((ZR, W), BF16), ((NZ, W // NZ, W), BF16)], [SM, VM, VM], flops=1 << 29, moved=1 << 20
    )(pole_weights, block, columns)
    quad = lax.all_to_all(quad, "z", 0, 0)
    mine, other = kernel_call(
        place_kernel, [((NX * NY, CAP, W), BF16)] * 2, [VM, VM], flops=1 << 23, moved=1 << 18
    )(block[:, 3 * RD :, :128], density)
    swap = ((0, 1), (1, 0))
    other = lax.ppermute(other, "c", swap)
    (joined,) = kernel_call(
        join_kernel, [((NX * NY, CAP, W + 128), BF16)], [SM, VM, VM, VM, VM], moved=1 << 18
    )(pole_weights, quad, diag_inverse, mine, other)
    joined = lax.all_to_all(joined, ("x", "y"), 0, 0)
    half, diag = kernel_call(total_kernel, [((CAP, W), BF16), ((2, W), F32)], [VM], moved=1 << 18)(joined)
    density_diag = diag + lax.ppermute(diag, "c", swap)
    patch_energy = jnp.dot(half, ham_slab, preferred_element_type=F32).astype(BF16)
    return (density_diag, patch_energy)


def solution(mesh):
    fine = Mesh(mesh.devices.reshape(NX, NC, NZ, NY), ("x", "c", "z", "y"))
    pole, grid = ("x", "c"), ("z", "y")
    by_row = P(pole, None, grid, None)
    return jax.shard_map(
        per_device,
        mesh=fine,
        in_specs=(by_row, by_row, by_row, P(pole, None), P(grid, None), P()),
        out_specs=(P(grid, None), P(("x", "c", "z", "y"), None)),
        check_vma=False,
    )
```

```python
import jax
import jax.numpy as jnp
from jax import lax
from jax.experimental import pallas as pl
from jax.experimental.pallas import tpu as pltpu
from jax.sharding import Mesh, PartitionSpec as P

NX, NC, NZ, NY = 4, 2, 16, 8
RD = 32
W = 256
ZR = NY * RD
YC = NZ * RD
CAP = 8
TAIL = 16
PIECE = 1024
F32 = jnp.float32
BF16 = jnp.bfloat16
VM = pl.BlockSpec(memory_space=pltpu.VMEM)
SM = pl.BlockSpec(memory_space=pltpu.SMEM)


def kernel_call(body, outs, specs, flops=0, moved=0, kept=(True, True), scratch=()):
    call = pl.pallas_call(
        body,
        out_shape=tuple(pltpu.VMEM(s, d) if k else jax.ShapeDtypeStruct(s, d) for (s, d), k in zip(outs, kept)),
        in_specs=specs,
        out_specs=tuple(VM for _ in outs),
        scratch_shapes=scratch,
        cost_estimate=pl.CostEstimate(flops=flops, bytes_accessed=moved, transcendentals=0),
    )

    def run(*args):
        return call(
            *(
                pltpu.with_memory_space_constraint(arg, pltpu.VMEM) if spec is VM else arg
                for arg, spec in zip(args, specs, strict=True)
            )
        )

    return run


def pack_kernel(o_hbm, g_hbm, l_hbm, out_hbm, own_ref, o_ref, g_ref, l_ref, out_ref, in_sem, out_sem):
    owners_in = pltpu.make_async_copy(o_hbm, o_ref, in_sem.at[0])
    rows_in = pltpu.make_async_copy(l_hbm, l_ref, in_sem.at[1])
    wide = NZ * W // 2
    pieces_in = [
        [
            pltpu.make_async_copy(
                g_hbm.at[0, part, :, pl.ds(wide * side, wide)],
                g_ref.at[part, :, pl.ds(wide * side, wide)],
                in_sem.at[2 + 2 * part + side],
            )
            for side in range(2)
        ]
        for part in range(2)
    ]
    spans = [(RD * part, RD, 256 * side, 256) for part in range(2) for side in range(2)] + [(2 * RD, RD + TAIL, 0, YC)]
    pieces_out = [
        pltpu.make_async_copy(
            out_ref.at[:, pl.ds(row, rows), pl.ds(lane, lanes)],
            out_hbm.at[:, pl.ds(row, rows), pl.ds(lane, lanes)],
            out_sem.at[i],
        )
        for i, (row, rows, lane, lanes) in enumerate(spans)
    ]
    owners_in.start()
    rows_in.start()
    for part in range(2):
        for side in range(2):
            pieces_in[part][side].start()
    rows_in.wait()
    for side in range(2):
        rows = l_ref[0, side]
        own_ref[:, W * side : W * side + W] = rows
        for y in range(NY):
            out_ref[y, 2 * RD : 3 * RD, W * side : W * side + W] = rows
    owners_in.wait()
    owner = jnp.broadcast_to(o_ref[...], (RD, RD))
    row = lax.broadcasted_iota(jnp.int32, (RD, RD), 0)
    column = lax.broadcasted_iota(jnp.int32, (RD, RD), 1)
    owner_down = jnp.sum(jnp.where(row == column, owner, 0), axis=1, keepdims=True)
    earlier = (owner_down == owner) & (row < column)
    rank = jnp.sum(earlier.astype(jnp.int32), axis=0, keepdims=True)
    slot = (o_ref[...] * CAP + rank).astype(F32)
    slot = jnp.broadcast_to(slot, (TAIL, RD)).astype(BF16)
    for y in range(NY):
        out_ref[y, 3 * RD :, :] = jnp.zeros((TAIL, YC), BF16)
        out_ref[y, 3 * RD :, 0:RD] = slot
    pieces_out[4].start()
    quarter = lax.broadcasted_iota(jnp.int32, (RD, 128), 1) // 32
    for part in range(2):
        for tile in range(4):
            if tile % 2 == 0:
                pieces_in[part][tile // 2].wait()
            for half in range(2):
                loaded = [
                    g_ref[part, :, (4 * tile + j) * W + half * 128 : (4 * tile + j) * W + half * 128 + 128].astype(F32)
                    for j in range(4)
                ]
                for q in range(4):
                    joined = None
                    for j in range(4):
                        shift = (32 * (j - q)) % 128
                        moved = pltpu.roll(loaded[j], shift, 1) if shift else loaded[j]
                        joined = moved if joined is None else jnp.where(quarter == j, moved, joined)
                    out_ref[4 * half + q, RD * part : RD * part + RD, 128 * tile : 128 * tile + 128] = joined.astype(BF16)
            if tile % 2 == 1:
                pieces_out[2 * part + tile // 2].start()
    for piece in pieces_out:
        piece.wait()


def pack(owner_map, trailing, panel):
    packed = (NY, 3 * RD + TAIL, YC)
    anywhere = pl.BlockSpec(memory_space=pl.ANY)
    return pl.pallas_call(
        pack_kernel,
        out_shape=(jax.ShapeDtypeStruct(packed, BF16), pltpu.VMEM((RD, 2 * W), BF16)),
        in_specs=[anywhere] * 3,
        out_specs=(anywhere, VM),
        scratch_shapes=[
            pltpu.VMEM((1, RD), jnp.int32),
            pltpu.VMEM((2, RD, NZ * W), BF16),
            pltpu.VMEM((1, 2, RD, W), BF16),
            pltpu.VMEM(packed, BF16),
            pltpu.SemaphoreType.DMA((6,)),
            pltpu.SemaphoreType.DMA((5,)),
        ],
        name="pack",
        cost_estimate=pl.CostEstimate(flops=0, bytes_accessed=1 << 20, transcendentals=0),
    )(owner_map.reshape(1, RD), trailing, panel)


def cross_kernel(w_ref, b_ref, l_ref, density_ref, quad_ref):
    wr = w_ref[0, 0]
    wi = w_ref[0, 1]
    columns = l_ref[...].reshape(YC, 2 * W)
    first = jnp.dot(b_ref[:, 0:RD, :].reshape(ZR, YC), columns, preferred_element_type=F32)
    second = jnp.dot(b_ref[:, RD : 2 * RD, :].reshape(ZR, YC), columns, preferred_element_type=F32)
    real = first[:, :W] - second[:, W:]
    imag = first[:, W:] + second[:, :W]
    even = wr * imag + wi * real
    odd = wr * real - wi * imag
    rows = b_ref[:, 2 * RD : 3 * RD, :].reshape(ZR, 2 * W)
    over_rows = (((0,), (0,)), ((), ()))
    quad = lax.dot_general(rows[:, :W], even.astype(BF16), over_rows, preferred_element_type=F32)
    quad = quad + lax.dot_general(rows[:, W:], odd.astype(BF16), over_rows, preferred_element_type=F32)
    quad_ref[...] = quad.astype(BF16).reshape(NZ, W // NZ, W)
    density_ref[...] = (-even).astype(BF16)


def place_kernel(s_ref, density_ref, mine_ref, other_ref):
    core = lax.axis_index("c")
    line = lax.broadcasted_iota(jnp.int32, (2 * NX * CAP, RD), 0)
    half = line // (NX * CAP)
    within = line % (NX * CAP)
    side = jnp.where(half == 0, core, 1 - core)
    index = (within // CAP * NC + side) * CAP + within % CAP
    for y in range(NY):
        slot = s_ref[y, 0:1, 0:RD].astype(F32).astype(jnp.int32)
        place = (index == slot).astype(F32).astype(BF16)
        rows = density_ref[RD * y : RD * y + RD, :]
        placed = jnp.dot(place, rows, preferred_element_type=F32).astype(BF16)
        for x in range(NX):
            mine_ref[NY * x + y] = placed[CAP * x : CAP * x + CAP]
            other_ref[NY * x + y] = placed[CAP * (NX + x) : CAP * (NX + x) + CAP]


def join_kernel(w_ref, q_ref, d_ref, p_ref, o_ref, out_ref):
    quad = jnp.sum(q_ref[...].astype(F32), axis=0)
    diag = w_ref[0, 0] * d_ref[0, 1].astype(F32) + w_ref[0, 1] * d_ref[0, 0].astype(F32)
    here = lax.axis_index("y")
    zero = jnp.zeros((CAP - 4, 128), F32)
    out_ref[:, :, 0:W] = (p_ref[...].astype(F32) + o_ref[...].astype(F32)).astype(BF16)
    for y in range(NY):
        rows = quad[2 * y : 2 * y + 2] + jnp.where(here == y, diag, 0.0)
        tail = jnp.concatenate([rows[:, :128], rows[:, 128:], zero], axis=0).astype(BF16)
        for x in range(NX):
            out_ref[NY * x + y, :, W:] = tail


def total_kernel(p_ref, h_hbm, diag_ref, energy_ref, h_ref, sem):
    spans = [pl.ds(start, PIECE) for start in range(0, NZ * NY * RD, PIECE)]
    pieces = [pltpu.make_async_copy(h_hbm.at[:, span], h_ref.at[:, span], sem.at[i]) for i, span in enumerate(spans)]
    for piece in pieces:
        piece.start()
    total = jnp.sum(p_ref[...].astype(F32), axis=0)
    diag_ref[:, 0:128] = total[0:2, W:]
    diag_ref[:, 128:] = total[2:4, W:]
    half = total[:, :W].astype(BF16)
    for piece, span in zip(pieces, spans, strict=True):
        piece.wait()
        energy_ref[:, span] = jnp.dot(half, h_ref[:, span], preferred_element_type=F32).astype(BF16)


def per_device(trailing, panel, diag_inverse, pole_weights, owner_map, ham_slab):
    packed, own = pack(owner_map, trailing, panel)
    block = lax.all_to_all(packed, "y", 0, 0)
    columns = lax.all_gather(own, "z")
    density, quad = kernel_call(
        cross_kernel, [((ZR, W), BF16), ((NZ, W // NZ, W), BF16)], [SM, VM, VM], flops=1 << 29, moved=1 << 20
    )(pole_weights, block, columns)
    quad = lax.all_to_all(quad, "z", 0, 0)
    mine, other = kernel_call(
        place_kernel, [((NX * NY, CAP, W), BF16)] * 2, [VM, VM], flops=1 << 23, moved=1 << 18
    )(block[:, 3 * RD :, :128], density)
    swap = ((0, 1), (1, 0))
    other = lax.ppermute(other, "c", swap)
    (joined,) = kernel_call(
        join_kernel, [((NX * NY, CAP, W + 128), BF16)], [SM, VM, VM, VM, VM], moved=1 << 18
    )(pole_weights, quad, diag_inverse, mine, other)
    joined = lax.all_to_all(joined, ("x", "y"), 0, 0)
    diag, patch_energy = kernel_call(
        total_kernel,
        [((2, W), F32), ((CAP, NZ * NY * RD), BF16)],
        [VM, pl.BlockSpec(memory_space=pl.ANY)],
        flops=1 << 24,
        moved=1 << 21,
        kept=(True, False),
        scratch=[pltpu.VMEM((W, NZ * NY * RD), BF16), pltpu.SemaphoreType.DMA((NZ * NY * RD // PIECE,))],
    )(joined, ham_slab)
    density_diag = lax.psum(diag, "c")
    return (density_diag, patch_energy)


def solution(mesh):
    fine = Mesh(mesh.devices.reshape(NX, NC, NZ, NY), ("x", "c", "z", "y"))
    pole, grid = ("x", "c"), ("z", "y")
    by_row = P(pole, None, grid, None)
    return jax.shard_map(
        per_device,
        mesh=fine,
        in_specs=(by_row, by_row, by_row, P(pole, None), P(grid, None), P()),
        out_specs=(P(grid, None), P(("x", "c", "z", "y"), None)),
        check_vma=False,
    )
```

```python
import jax
import jax.numpy as jnp
from jax import lax
from jax.experimental import pallas as pl
from jax.experimental.pallas import tpu as pltpu
from jax.sharding import Mesh, PartitionSpec as P

NX, NC, NZ, NY = 4, 2, 16, 8
RD = 32
W = 256
ZR = NY * RD
YC = NZ * RD
CAP = 8
TAIL = 16
HOLD = 1
HELD = 3072
PIECE = 1024
F32 = jnp.float32
BF16 = jnp.bfloat16
VM = pl.BlockSpec(memory_space=pltpu.VMEM)
SM = pl.BlockSpec(memory_space=pltpu.SMEM)


def kernel_call(body, outs, specs, flops=0, moved=0, kept=(True,) * 8, scratch=()):
    call = pl.pallas_call(
        body,
        out_shape=tuple(pltpu.VMEM(s, d) if k else jax.ShapeDtypeStruct(s, d) for (s, d), k in zip(outs, kept)),
        in_specs=specs,
        out_specs=tuple(VM for _ in outs),
        scratch_shapes=scratch,
        cost_estimate=pl.CostEstimate(flops=flops, bytes_accessed=moved, transcendentals=0),
    )

    def run(*args):
        return call(
            *(
                pltpu.with_memory_space_constraint(arg, pltpu.VMEM) if spec is VM else arg
                for arg, spec in zip(args, specs, strict=True)
            )
        )

    return run


def pack_kernel(o_hbm, g_hbm, l_hbm, out_hbm, own_ref, o_ref, g_ref, l_ref, out_ref, in_sem, out_sem):
    owners_in = pltpu.make_async_copy(o_hbm, o_ref, in_sem.at[0])
    rows_in = pltpu.make_async_copy(l_hbm, l_ref, in_sem.at[1])
    wide = NZ * W // 2
    pieces_in = [
        [
            pltpu.make_async_copy(
                g_hbm.at[0, part, :, pl.ds(wide * side, wide)],
                g_ref.at[part, :, pl.ds(wide * side, wide)],
                in_sem.at[2 + 2 * part + side],
            )
            for side in range(2)
        ]
        for part in range(2)
    ]
    spans = [(RD * part, RD, 256 * side, 256) for part in range(2) for side in range(2)] + [(2 * RD, RD + TAIL, 0, YC)]
    pieces_out = [
        pltpu.make_async_copy(
            out_ref.at[:, pl.ds(row, rows), pl.ds(lane, lanes)],
            out_hbm.at[:, pl.ds(row, rows), pl.ds(lane, lanes)],
            out_sem.at[i],
        )
        for i, (row, rows, lane, lanes) in enumerate(spans)
    ]
    owners_in.start()
    rows_in.start()
    for part in range(2):
        for side in range(2):
            pieces_in[part][side].start()
    rows_in.wait()
    for side in range(2):
        rows = l_ref[0, side]
        own_ref[:, W * side : W * side + W] = rows
        for y in range(NY):
            out_ref[y, 2 * RD : 3 * RD, W * side : W * side + W] = rows
    owners_in.wait()
    owner = jnp.broadcast_to(o_ref[...], (RD, RD))
    row = lax.broadcasted_iota(jnp.int32, (RD, RD), 0)
    column = lax.broadcasted_iota(jnp.int32, (RD, RD), 1)
    owner_down = jnp.sum(jnp.where(row == column, owner, 0), axis=1, keepdims=True)
    earlier = (owner_down == owner) & (row < column)
    rank = jnp.sum(earlier.astype(jnp.int32), axis=0, keepdims=True)
    slot = (o_ref[...] * CAP + rank).astype(F32)
    slot = jnp.broadcast_to(slot, (TAIL, RD)).astype(BF16)
    for y in range(NY):
        out_ref[y, 3 * RD :, :] = jnp.zeros((TAIL, YC), BF16)
        out_ref[y, 3 * RD :, 0:RD] = slot
    pieces_out[4].start()
    quarter = lax.broadcasted_iota(jnp.int32, (RD, 128), 1) // 32
    for part in range(2):
        for tile in range(4):
            if tile % 2 == 0:
                pieces_in[part][tile // 2].wait()
            for half in range(2):
                loaded = [
                    g_ref[part, :, (4 * tile + j) * W + half * 128 : (4 * tile + j) * W + half * 128 + 128].astype(F32)
                    for j in range(4)
                ]
                for q in range(4):
                    joined = None
                    for j in range(4):
                        shift = (32 * (j - q)) % 128
                        moved = pltpu.roll(loaded[j], shift, 1) if shift else loaded[j]
                        joined = moved if joined is None else jnp.where(quarter == j, moved, joined)
                    out_ref[4 * half + q, RD * part : RD * part + RD, 128 * tile : 128 * tile + 128] = joined.astype(BF16)
            if tile % 2 == 1:
                pieces_out[2 * part + tile // 2].start()
    for piece in pieces_out:
        piece.wait()


def pack(owner_map, trailing, panel):
    packed = (NY, 3 * RD + TAIL, YC)
    anywhere = pl.BlockSpec(memory_space=pl.ANY)
    return pl.pallas_call(
        pack_kernel,
        out_shape=(jax.ShapeDtypeStruct(packed, BF16), pltpu.VMEM((RD, 2 * W), BF16)),
        in_specs=[anywhere] * 3,
        out_specs=(anywhere, VM),
        scratch_shapes=[
            pltpu.VMEM((1, RD), jnp.int32),
            pltpu.VMEM((2, RD, NZ * W), BF16),
            pltpu.VMEM((1, 2, RD, W), BF16),
            pltpu.VMEM(packed, BF16),
            pltpu.SemaphoreType.DMA((6,)),
            pltpu.SemaphoreType.DMA((5,)),
        ],
        name="pack",
        cost_estimate=pl.CostEstimate(flops=0, bytes_accessed=1 << 20, transcendentals=0),
    )(owner_map.reshape(1, RD), trailing, panel)


def cross_kernel(w_ref, b_ref, l_ref, density_ref, quad_ref):
    wr = w_ref[0, 0]
    wi = w_ref[0, 1]
    columns = l_ref[...].reshape(YC, 2 * W)
    first = jnp.dot(b_ref[:, 0:RD, :].reshape(ZR, YC), columns, preferred_element_type=F32)
    second = jnp.dot(b_ref[:, RD : 2 * RD, :].reshape(ZR, YC), columns, preferred_element_type=F32)
    real = first[:, :W] - second[:, W:]
    imag = first[:, W:] + second[:, :W]
    even = wr * imag + wi * real
    odd = wr * real - wi * imag
    rows = b_ref[:, 2 * RD : 3 * RD, :].reshape(ZR, 2 * W)
    over_rows = (((0,), (0,)), ((), ()))
    quad = lax.dot_general(rows[:, :W], even.astype(BF16), over_rows, preferred_element_type=F32)
    quad = quad + lax.dot_general(rows[:, W:], odd.astype(BF16), over_rows, preferred_element_type=F32)
    quad_ref[...] = quad.astype(BF16).reshape(NZ, W // NZ, W)
    density_ref[...] = (-even).astype(BF16)


def place_kernel(s_ref, d_ref, o_ref, h_hbm, out_ref, *rest):
    slabs, sem = rest[:-1], rest[-1]
    pieces = [
        pltpu.make_async_copy(h_hbm.at[:, pl.ds(HELD * i, HELD)], slab, sem.at[i]) for i, slab in enumerate(slabs)
    ]
    for piece in pieces:
        piece.start()
    line = lax.broadcasted_iota(jnp.int32, (NX * CAP, RD), 0)
    index = (line // CAP * NC + lax.axis_index("c")) * CAP + line % CAP
    rows = (d_ref[...].astype(F32) + o_ref[...].astype(F32)).astype(BF16)
    for y in range(NY):
        slot = s_ref[y, 0:1, 0:RD].astype(F32).astype(jnp.int32)
        place = (index == slot).astype(F32).astype(BF16)
        placed = jnp.dot(place, rows[RD * y : RD * y + RD], preferred_element_type=F32).astype(BF16)
        for x in range(NX):
            out_ref[NY * x + y] = placed[CAP * x : CAP * x + CAP]
    for piece in pieces:
        piece.wait()


def join_kernel(w_ref, q_ref, d_ref, p_ref, out_ref):
    quad = jnp.sum(q_ref[...].astype(F32), axis=0)
    diag = w_ref[0, 0] * d_ref[0, 1].astype(F32) + w_ref[0, 1] * d_ref[0, 0].astype(F32)
    here = lax.axis_index("y")
    zero = jnp.zeros((CAP - 4, 128), F32)
    out_ref[:, :, 0:W] = p_ref[...]
    for y in range(NY):
        rows = quad[2 * y : 2 * y + 2] + jnp.where(here == y, diag, 0.0)
        tail = jnp.concatenate([rows[:, :128], rows[:, 128:], zero], axis=0).astype(BF16)
        for x in range(NX):
            out_ref[NY * x + y, :, W:] = tail


def total_kernel(p_ref, *refs):
    slabs, (h_hbm, diag_ref, energy_ref, h_ref, sem) = refs[:HOLD], refs[HOLD:]
    held = HOLD * HELD
    spans = [pl.ds(start, PIECE) for start in range(0, NZ * NY * RD - held, PIECE)]
    pieces = [
        pltpu.make_async_copy(h_hbm.at[:, pl.ds(held + PIECE * i, PIECE)], h_ref.at[:, span], sem.at[i])
        for i, span in enumerate(spans)
    ]
    for piece in pieces:
        piece.start()
    total = jnp.sum(p_ref[...].astype(F32), axis=0)
    diag_ref[:, 0:128] = total[0:2, W:]
    diag_ref[:, 128:] = total[2:4, W:]
    half = total[:, :W].astype(BF16)
    for i, slab in enumerate(slabs):
        span = pl.ds(HELD * i, HELD)
        energy_ref[:, span] = jnp.dot(half, slab[...], preferred_element_type=F32).astype(BF16)
    for i, (piece, span) in enumerate(zip(pieces, spans, strict=True)):
        piece.wait()
        to = pl.ds(held + PIECE * i, PIECE)
        energy_ref[:, to] = jnp.dot(half, h_ref[:, span], preferred_element_type=F32).astype(BF16)


def per_device(trailing, panel, diag_inverse, pole_weights, owner_map, ham_slab):
    packed, own = pack(owner_map, trailing, panel)
    block = lax.all_to_all(packed, "y", 0, 0)
    columns = lax.all_gather(own, "z")
    density, quad = kernel_call(
        cross_kernel, [((ZR, W), BF16), ((NZ, W // NZ, W), BF16)], [SM, VM, VM], flops=1 << 29, moved=1 << 20
    )(pole_weights, block, columns)
    quad = lax.all_to_all(quad, "z", 0, 0)
    other = lax.ppermute(density, "c", ((0, 1), (1, 0)))
    placed, *slabs = kernel_call(
        place_kernel,
        [((NX * NY, CAP, W), BF16)] + [((W, HELD), BF16)] * HOLD,
        [VM, VM, VM, pl.BlockSpec(memory_space=pl.ANY)],
        flops=1 << 23,
        moved=1 << 21,
        scratch=[pltpu.SemaphoreType.DMA((HOLD,))],
    )(block[:, 3 * RD :, :128], density, other, ham_slab)
    (joined,) = kernel_call(
        join_kernel, [((NX * NY, CAP, W + 128), BF16)], [SM, VM, VM, VM], moved=1 << 18
    )(pole_weights, quad, diag_inverse, placed)
    joined = lax.all_to_all(joined, ("x", "y"), 0, 0)
    streamed = NZ * NY * RD - HOLD * HELD
    diag, patch_energy = kernel_call(
        total_kernel,
        [((2, W), F32), ((CAP, NZ * NY * RD), BF16)],
        [VM] * (1 + HOLD) + [pl.BlockSpec(memory_space=pl.ANY)],
        flops=1 << 24,
        moved=1 << 18,
        kept=(True, False),
        scratch=[pltpu.VMEM((W, streamed), BF16), pltpu.SemaphoreType.DMA((streamed // PIECE,))],
    )(joined, *slabs, ham_slab)
    density_diag = lax.psum(diag, "c")
    return (density_diag, patch_energy)


def solution(mesh):
    fine = Mesh(mesh.devices.reshape(NX, NC, NZ, NY), ("x", "c", "z", "y"))
    pole, grid = ("x", "c"), ("z", "y")
    by_row = P(pole, None, grid, None)
    return jax.shard_map(
        per_device,
        mesh=fine,
        in_specs=(by_row, by_row, by_row, P(pole, None), P(grid, None), P()),
        out_specs=(P(grid, None), P(("x", "c", "z", "y"), None)),
        check_vma=False,
    )
```

```python
import jax
import jax.numpy as jnp
from jax import lax
from jax.experimental import pallas as pl
from jax.experimental.pallas import tpu as pltpu
from jax.sharding import Mesh, PartitionSpec as P

NX, NC, NZ, NY = 4, 2, 16, 8
RD = 32
W = 256
ZR = NY * RD
YC = NZ * RD
CAP = 8
TAIL = 16
HOLD = 1
HELD = 3072
PIECE = 1024
F32 = jnp.float32
BF16 = jnp.bfloat16
VM = pl.BlockSpec(memory_space=pltpu.VMEM)
SM = pl.BlockSpec(memory_space=pltpu.SMEM)


def kernel_call(body, outs, specs, flops=0, moved=0, kept=(True,) * 8, scratch=()):
    call = pl.pallas_call(
        body,
        out_shape=tuple(pltpu.VMEM(s, d) if k else jax.ShapeDtypeStruct(s, d) for (s, d), k in zip(outs, kept)),
        in_specs=specs,
        out_specs=tuple(VM for _ in outs),
        scratch_shapes=scratch,
        cost_estimate=pl.CostEstimate(flops=flops, bytes_accessed=moved, transcendentals=0),
    )

    def run(*args):
        return call(
            *(
                pltpu.with_memory_space_constraint(arg, pltpu.VMEM) if spec is VM else arg
                for arg, spec in zip(args, specs, strict=True)
            )
        )

    return run


def pack_kernel(o_hbm, g_hbm, l_hbm, out_hbm, own_ref, o_ref, g_ref, l_ref, out_ref, in_sem, out_sem):
    owners_in = pltpu.make_async_copy(o_hbm, o_ref, in_sem.at[0])
    rows_in = pltpu.make_async_copy(l_hbm, l_ref, in_sem.at[1])
    wide = NZ * W // 2
    pieces_in = [
        [
            pltpu.make_async_copy(
                g_hbm.at[0, part, :, pl.ds(wide * side, wide)],
                g_ref.at[part, :, pl.ds(wide * side, wide)],
                in_sem.at[2 + 2 * part + side],
            )
            for side in range(2)
        ]
        for part in range(2)
    ]
    spans = [(RD * part, RD, 256 * side, 256) for part in range(2) for side in range(2)] + [(2 * RD, RD + TAIL, 0, YC)]
    pieces_out = [
        pltpu.make_async_copy(
            out_ref.at[:, pl.ds(row, rows), pl.ds(lane, lanes)],
            out_hbm.at[:, pl.ds(row, rows), pl.ds(lane, lanes)],
            out_sem.at[i],
        )
        for i, (row, rows, lane, lanes) in enumerate(spans)
    ]
    owners_in.start()
    rows_in.start()
    for part in range(2):
        for side in range(2):
            pieces_in[part][side].start()
    rows_in.wait()
    for side in range(2):
        rows = l_ref[0, side]
        own_ref[:, W * side : W * side + W] = rows
        for y in range(NY):
            out_ref[y, 2 * RD : 3 * RD, W * side : W * side + W] = rows
    owners_in.wait()
    owner = jnp.broadcast_to(o_ref[...], (RD, RD))
    row = lax.broadcasted_iota(jnp.int32, (RD, RD), 0)
    column = lax.broadcasted_iota(jnp.int32, (RD, RD), 1)
    owner_down = jnp.sum(jnp.where(row == column, owner, 0), axis=1, keepdims=True)
    earlier = (owner_down == owner) & (row < column)
    rank = jnp.sum(earlier.astype(jnp.int32), axis=0, keepdims=True)
    slot = (o_ref[...] * CAP + rank).astype(F32)
    slot = jnp.broadcast_to(slot, (TAIL, RD)).astype(BF16)
    for y in range(NY):
        out_ref[y, 3 * RD :, :] = jnp.zeros((TAIL, YC), BF16)
        out_ref[y, 3 * RD :, 0:RD] = slot
    pieces_out[4].start()
    quarter = lax.broadcasted_iota(jnp.int32, (RD, 128), 1) // 32
    for part in range(2):
        for tile in range(4):
            if tile % 2 == 0:
                pieces_in[part][tile // 2].wait()
            for half in range(2):
                loaded = [
                    g_ref[part, :, (4 * tile + j) * W + half * 128 : (4 * tile + j) * W + half * 128 + 128].astype(F32)
                    for j in range(4)
                ]
                for q in range(4):
                    joined = None
                    for j in range(4):
                        shift = (32 * (j - q)) % 128
                        moved = pltpu.roll(loaded[j], shift, 1) if shift else loaded[j]
                        joined = moved if joined is None else jnp.where(quarter == j, moved, joined)
                    out_ref[4 * half + q, RD * part : RD * part + RD, 128 * tile : 128 * tile + 128] = joined.astype(BF16)
            if tile % 2 == 1:
                pieces_out[2 * part + tile // 2].start()
    for piece in pieces_out:
        piece.wait()


def pack(owner_map, trailing, panel):
    packed = (NY, 3 * RD + TAIL, YC)
    anywhere = pl.BlockSpec(memory_space=pl.ANY)
    return pl.pallas_call(
        pack_kernel,
        out_shape=(jax.ShapeDtypeStruct(packed, BF16), pltpu.VMEM((RD, 2 * W), BF16)),
        in_specs=[anywhere] * 3,
        out_specs=(anywhere, VM),
        scratch_shapes=[
            pltpu.VMEM((1, RD), jnp.int32),
            pltpu.VMEM((2, RD, NZ * W), BF16),
            pltpu.VMEM((1, 2, RD, W), BF16),
            pltpu.VMEM(packed, BF16),
            pltpu.SemaphoreType.DMA((6,)),
            pltpu.SemaphoreType.DMA((5,)),
        ],
        name="pack",
        cost_estimate=pl.CostEstimate(flops=0, bytes_accessed=1 << 20, transcendentals=0),
    )(owner_map.reshape(1, RD), trailing, panel)


def cross_kernel(w_ref, b_ref, l_ref, d_ref, out_ref):
    wr = w_ref[0, 0]
    wi = w_ref[0, 1]
    columns = l_ref[...].reshape(YC, 2 * W)
    first = jnp.dot(b_ref[:, 0:RD, :].reshape(ZR, YC), columns, preferred_element_type=F32)
    second = jnp.dot(b_ref[:, RD : 2 * RD, :].reshape(ZR, YC), columns, preferred_element_type=F32)
    real = first[:, :W] - second[:, W:]
    imag = first[:, W:] + second[:, :W]
    even = wr * imag + wi * real
    odd = wr * real - wi * imag
    rows = b_ref[:, 2 * RD : 3 * RD, :].reshape(ZR, 2 * W)
    over_rows = (((0,), (0,)), ((), ()))
    quad = lax.dot_general(rows[:, :W], even.astype(BF16), over_rows, preferred_element_type=F32)
    quad = quad + lax.dot_general(rows[:, W:], odd.astype(BF16), over_rows, preferred_element_type=F32)
    diag = wr * d_ref[0, 1].astype(F32) + wi * d_ref[0, 0].astype(F32)
    at = lax.axis_index("z") * (2 * NY) + lax.axis_index("y") * 2
    line = lax.broadcasted_iota(jnp.int32, (W, W), 0)
    for row in range(2):
        quad = quad + jnp.where(line == at + row, diag[row : row + 1], 0.0)
    out_ref[:, 0:W] = (-even).astype(BF16)
    out_ref[:, W:] = quad.astype(BF16)


def pair_kernel(p_ref, density_ref, quad_ref):
    quad_ref[...] = (p_ref[0, :, W:].astype(F32) + p_ref[1, :, W:].astype(F32)).astype(BF16).reshape(NZ, W // NZ, W)
    density_ref[...] = (p_ref[0, :, 0:W].astype(F32) + p_ref[1, :, 0:W].astype(F32)).astype(BF16)


def place_kernel(s_ref, d_ref, h_hbm, out_ref, *rest):
    slabs, sem = rest[:-1], rest[-1]
    pieces = [
        pltpu.make_async_copy(h_hbm.at[:, pl.ds(HELD * i, HELD)], slab, sem.at[i]) for i, slab in enumerate(slabs)
    ]
    for piece in pieces:
        piece.start()
    line = lax.broadcasted_iota(jnp.int32, (NX * CAP, RD), 0)
    index = (line // CAP * NC + lax.axis_index("c")) * CAP + line % CAP
    rows = d_ref[...]
    for y in range(NY):
        slot = s_ref[y, 0:1, 0:RD].astype(F32).astype(jnp.int32)
        place = (index == slot).astype(F32).astype(BF16)
        placed = jnp.dot(place, rows[RD * y : RD * y + RD], preferred_element_type=F32).astype(BF16)
        for x in range(NX):
            out_ref[NY * x + y] = placed[CAP * x : CAP * x + CAP]
    for piece in pieces:
        piece.wait()


def join_kernel(q_ref, p_ref, out_ref):
    quad = jnp.sum(q_ref[...].astype(F32), axis=0)
    zero = jnp.zeros((CAP - 4, 128), F32)
    out_ref[:, :, 0:W] = p_ref[...]
    for y in range(NY):
        rows = quad[2 * y : 2 * y + 2]
        tail = jnp.concatenate([rows[:, :128], rows[:, 128:], zero], axis=0).astype(BF16)
        for x in range(NX):
            out_ref[NY * x + y, :, W:] = tail


def total_kernel(p_ref, *refs):
    slabs, (h_hbm, diag_ref, energy_ref, h_ref, sem) = refs[:HOLD], refs[HOLD:]
    held = HOLD * HELD
    spans = [pl.ds(start, PIECE) for start in range(0, NZ * NY * RD - held, PIECE)]
    pieces = [
        pltpu.make_async_copy(h_hbm.at[:, pl.ds(held + PIECE * i, PIECE)], h_ref.at[:, span], sem.at[i])
        for i, span in enumerate(spans)
    ]
    for piece in pieces:
        piece.start()
    total = jnp.sum(p_ref[...].astype(F32), axis=0)
    diag_ref[:, 0:128] = total[0:2, W:]
    diag_ref[:, 128:] = total[2:4, W:]
    half = total[:, :W].astype(BF16)
    for i, slab in enumerate(slabs):
        span = pl.ds(HELD * i, HELD)
        energy_ref[:, span] = jnp.dot(half, slab[...], preferred_element_type=F32).astype(BF16)
    for i, (piece, span) in enumerate(zip(pieces, spans, strict=True)):
        piece.wait()
        to = pl.ds(held + PIECE * i, PIECE)
        energy_ref[:, to] = jnp.dot(half, h_ref[:, span], preferred_element_type=F32).astype(BF16)


def per_device(trailing, panel, diag_inverse, pole_weights, owner_map, ham_slab):
    packed, own = pack(owner_map, trailing, panel)
    block = lax.all_to_all(packed, "y", 0, 0)
    columns = lax.all_gather(own, "z")
    (partial,) = kernel_call(
        cross_kernel, [((ZR, 2 * W), BF16)], [SM, VM, VM, VM], flops=1 << 29, moved=1 << 20
    )(pole_weights, block, columns, diag_inverse)
    both = lax.all_gather(partial, "c")
    density, quad = kernel_call(pair_kernel, [((ZR, W), BF16), ((NZ, W // NZ, W), BF16)], [VM], moved=1 << 19)(both)
    quad = lax.all_to_all(quad, "z", 0, 0)
    placed, *slabs = kernel_call(
        place_kernel,
        [((NX * NY, CAP, W), BF16)] + [((W, HELD), BF16)] * HOLD,
        [VM, VM, pl.BlockSpec(memory_space=pl.ANY)],
        flops=1 << 23,
        moved=1 << 21,
        scratch=[pltpu.SemaphoreType.DMA((HOLD,))],
    )(block[:, 3 * RD :, :128], density, ham_slab)
    (joined,) = kernel_call(join_kernel, [((NX * NY, CAP, W + 128), BF16)], [VM, VM], moved=1 << 18)(quad, placed)
    joined = lax.all_to_all(joined, ("x", "y"), 0, 0)
    streamed = NZ * NY * RD - HOLD * HELD
    density_diag, patch_energy = kernel_call(
        total_kernel,
        [((2, W), F32), ((CAP, NZ * NY * RD), BF16)],
        [VM] * (1 + HOLD) + [pl.BlockSpec(memory_space=pl.ANY)],
        flops=1 << 24,
        moved=1 << 18,
        kept=(False, False),
        scratch=[pltpu.VMEM((W, streamed), BF16), pltpu.SemaphoreType.DMA((streamed // PIECE,))],
    )(joined, *slabs, ham_slab)
    return (density_diag, patch_energy)


def solution(mesh):
    fine = Mesh(mesh.devices.reshape(NX, NC, NZ, NY), ("x", "c", "z", "y"))
    pole, grid = ("x", "c"), ("z", "y")
    by_row = P(pole, None, grid, None)
    return jax.shard_map(
        per_device,
        mesh=fine,
        in_specs=(by_row, by_row, by_row, P(pole, None), P(grid, None), P()),
        out_specs=(P(grid, None), P(("x", "c", "z", "y"), None)),
        check_vma=False,
    )
```

```python
import jax
import jax.numpy as jnp
from jax import lax
from jax.experimental import pallas as pl
from jax.experimental.pallas import tpu as pltpu
from jax.sharding import Mesh, PartitionSpec as P

NX, NC, NZ, NY = 4, 2, 16, 8
RD = 32
W = 256
ZR = NY * RD
YC = NZ * RD
CAP = 8
TAIL = 16
HOLD = 1
HELD = 3072
PIECE = 1024
F32 = jnp.float32
BF16 = jnp.bfloat16
VM = pl.BlockSpec(memory_space=pltpu.VMEM)
SM = pl.BlockSpec(memory_space=pltpu.SMEM)


def kernel_call(body, outs, specs, flops=0, moved=0, kept=(True,) * 8, scratch=()):
    call = pl.pallas_call(
        body,
        out_shape=tuple(pltpu.VMEM(s, d) if k else jax.ShapeDtypeStruct(s, d) for (s, d), k in zip(outs, kept)),
        in_specs=specs,
        out_specs=tuple(VM for _ in outs),
        scratch_shapes=scratch,
        cost_estimate=pl.CostEstimate(flops=flops, bytes_accessed=moved, transcendentals=0),
    )

    def run(*args):
        return call(
            *(
                pltpu.with_memory_space_constraint(arg, pltpu.VMEM) if spec is VM else arg
                for arg, spec in zip(args, specs, strict=True)
            )
        )

    return run


def pack_kernel(o_hbm, g_hbm, l_hbm, out_hbm, own_ref, o_ref, g_ref, l_ref, out_ref, in_sem, out_sem):
    owners_in = pltpu.make_async_copy(o_hbm, o_ref, in_sem.at[0])
    rows_in = pltpu.make_async_copy(l_hbm, l_ref, in_sem.at[1])
    wide = NZ * W // 2
    pieces_in = [
        [
            pltpu.make_async_copy(
                g_hbm.at[0, part, :, pl.ds(wide * side, wide)],
                g_ref.at[part, :, pl.ds(wide * side, wide)],
                in_sem.at[2 + 2 * part + side],
            )
            for side in range(2)
        ]
        for part in range(2)
    ]
    spans = [(RD * part, RD, 256 * side, 256) for part in range(2) for side in range(2)] + [(2 * RD, RD + TAIL, 0, YC)]
    pieces_out = [
        pltpu.make_async_copy(
            out_ref.at[:, pl.ds(row, rows), pl.ds(lane, lanes)],
            out_hbm.at[:, pl.ds(row, rows), pl.ds(lane, lanes)],
            out_sem.at[i],
        )
        for i, (row, rows, lane, lanes) in enumerate(spans)
    ]
    owners_in.start()
    rows_in.start()
    for part in range(2):
        for side in range(2):
            pieces_in[part][side].start()
    rows_in.wait()
    for side in range(2):
        rows = l_ref[0, side]
        own_ref[0, :, W * side : W * side + W] = rows
        for y in range(NY):
            out_ref[y, 2 * RD : 3 * RD, W * side : W * side + W] = rows
    owners_in.wait()
    owner = jnp.broadcast_to(o_ref[...], (RD, RD))
    row = lax.broadcasted_iota(jnp.int32, (RD, RD), 0)
    column = lax.broadcasted_iota(jnp.int32, (RD, RD), 1)
    owner_down = jnp.sum(jnp.where(row == column, owner, 0), axis=1, keepdims=True)
    earlier = (owner_down == owner) & (row < column)
    rank = jnp.sum(earlier.astype(jnp.int32), axis=0, keepdims=True)
    slot = (o_ref[...] * CAP + rank).astype(F32)
    slot = jnp.broadcast_to(slot, (TAIL, RD)).astype(BF16)
    for y in range(NY):
        out_ref[y, 3 * RD :, :] = jnp.zeros((TAIL, YC), BF16)
        out_ref[y, 3 * RD :, 0:RD] = slot
    pieces_out[4].start()
    quarter = lax.broadcasted_iota(jnp.int32, (RD, 128), 1) // 32
    for part in range(2):
        for tile in range(4):
            if tile % 2 == 0:
                pieces_in[part][tile // 2].wait()
            for half in range(2):
                loaded = [
                    g_ref[part, :, (4 * tile + j) * W + half * 128 : (4 * tile + j) * W + half * 128 + 128].astype(F32)
                    for j in range(4)
                ]
                for q in range(4):
                    joined = None
                    for j in range(4):
                        shift = (32 * (j - q)) % 128
                        moved = pltpu.roll(loaded[j], shift, 1) if shift else loaded[j]
                        joined = moved if joined is None else jnp.where(quarter == j, moved, joined)
                    out_ref[4 * half + q, RD * part : RD * part + RD, 128 * tile : 128 * tile + 128] = joined.astype(BF16)
            if tile % 2 == 1:
                pieces_out[2 * part + tile // 2].start()
    for piece in pieces_out:
        piece.wait()


def pack(owner_map, trailing, panel):
    packed = (NY, 3 * RD + TAIL, YC)
    anywhere = pl.BlockSpec(memory_space=pl.ANY)
    return pl.pallas_call(
        pack_kernel,
        out_shape=(jax.ShapeDtypeStruct(packed, BF16), pltpu.VMEM((1, RD, 2 * W), BF16)),
        in_specs=[anywhere] * 3,
        out_specs=(anywhere, VM),
        scratch_shapes=[
            pltpu.VMEM((1, RD), jnp.int32),
            pltpu.VMEM((2, RD, NZ * W), BF16),
            pltpu.VMEM((1, 2, RD, W), BF16),
            pltpu.VMEM(packed, BF16),
            pltpu.SemaphoreType.DMA((6,)),
            pltpu.SemaphoreType.DMA((5,)),
        ],
        name="pack",
        cost_estimate=pl.CostEstimate(flops=0, bytes_accessed=1 << 20, transcendentals=0),
    )(owner_map.reshape(1, RD), trailing, panel)


def cross_kernel(w_ref, b_ref, l_ref, d_ref, out_ref):
    wr = w_ref[0, 0]
    wi = w_ref[0, 1]
    columns = l_ref[...].reshape(YC, 2 * W)
    first = jnp.dot(b_ref[:, 0:RD, :].reshape(ZR, YC), columns, preferred_element_type=F32)
    second = jnp.dot(b_ref[:, RD : 2 * RD, :].reshape(ZR, YC), columns, preferred_element_type=F32)
    real = first[:, :W] - second[:, W:]
    imag = first[:, W:] + second[:, :W]
    even = wr * imag + wi * real
    odd = wr * real - wi * imag
    rows = b_ref[:, 2 * RD : 3 * RD, :].reshape(ZR, 2 * W)
    over_rows = (((0,), (0,)), ((), ()))
    quad = lax.dot_general(rows[:, :W], even.astype(BF16), over_rows, preferred_element_type=F32)
    quad = quad + lax.dot_general(rows[:, W:], odd.astype(BF16), over_rows, preferred_element_type=F32)
    diag = wr * d_ref[0, 1].astype(F32) + wi * d_ref[0, 0].astype(F32)
    at = lax.axis_index("z") * (2 * NY) + lax.axis_index("y") * 2
    line = lax.broadcasted_iota(jnp.int32, (W, W), 0)
    for row in range(2):
        quad = quad + jnp.where(line == at + row, diag[row : row + 1], 0.0)
    out_ref[:, 0:W] = (-even).astype(BF16)
    out_ref[:, W:] = quad.astype(BF16)


def pair_kernel(p_ref, density_ref, quad_ref):
    quad_ref[...] = (p_ref[0, :, W:].astype(F32) + p_ref[1, :, W:].astype(F32)).astype(BF16).reshape(NZ, W // NZ, W)
    density_ref[...] = (p_ref[0, :, 0:W].astype(F32) + p_ref[1, :, 0:W].astype(F32)).astype(BF16)


def place_kernel(s_ref, d_ref, h_hbm, out_ref, *rest):
    slabs, sem = rest[:-1], rest[-1]
    pieces = [
        pltpu.make_async_copy(h_hbm.at[:, pl.ds(HELD * i, HELD)], slab, sem.at[i]) for i, slab in enumerate(slabs)
    ]
    for piece in pieces:
        piece.start()
    line = lax.broadcasted_iota(jnp.int32, (NX * CAP, RD), 0)
    index = (line // CAP * NC + lax.axis_index("c")) * CAP + line % CAP
    rows = d_ref[...]
    for y in range(NY):
        slot = s_ref[y, 0:1, 0:RD].astype(F32).astype(jnp.int32)
        place = (index == slot).astype(F32).astype(BF16)
        placed = jnp.dot(place, rows[RD * y : RD * y + RD], preferred_element_type=F32).astype(BF16)
        for x in range(NX):
            for part in range(2):
                start = CAP * x + 4 * part
                out_ref[NY * x + y, :, W * part : W * part + W] = placed[start : start + 4]
    for piece in pieces:
        piece.wait()


def join_kernel(q_ref, p_ref, out_ref):
    quad = jnp.sum(q_ref[...].astype(F32), axis=0)
    out_ref[:, :, 0 : 2 * W] = p_ref[...]
    for y in range(NY):
        rows = quad[2 * y : 2 * y + 2]
        tail = jnp.concatenate([rows[:, :128], rows[:, 128:]], axis=0).astype(BF16)
        for x in range(NX):
            out_ref[NY * x + y, :, 2 * W :] = tail


def total_kernel(p_ref, *refs):
    slabs, (h_hbm, diag_ref, energy_ref, h_ref, sem) = refs[:HOLD], refs[HOLD:]
    held = HOLD * HELD
    spans = [pl.ds(start, PIECE) for start in range(0, NZ * NY * RD - held, PIECE)]
    pieces = [
        pltpu.make_async_copy(h_hbm.at[:, pl.ds(held + PIECE * i, PIECE)], h_ref.at[:, span], sem.at[i])
        for i, span in enumerate(spans)
    ]
    for piece in pieces:
        piece.start()
    total = jnp.sum(p_ref[...].astype(F32), axis=0)
    diag_ref[:, 0:128] = total[0:2, 2 * W :]
    diag_ref[:, 128:] = total[2:4, 2 * W :]
    half = jnp.concatenate([total[:, :W], total[:, W : 2 * W]], axis=0).astype(BF16)
    for i, slab in enumerate(slabs):
        span = pl.ds(HELD * i, HELD)
        energy_ref[:, span] = jnp.dot(half, slab[...], preferred_element_type=F32).astype(BF16)
    for i, (piece, span) in enumerate(zip(pieces, spans, strict=True)):
        piece.wait()
        to = pl.ds(held + PIECE * i, PIECE)
        energy_ref[:, to] = jnp.dot(half, h_ref[:, span], preferred_element_type=F32).astype(BF16)


def per_device(trailing, panel, diag_inverse, pole_weights, owner_map, ham_slab):
    packed, own = pack(owner_map, trailing, panel)
    block = lax.all_to_all(packed, "y", 0, 0)
    columns = lax.all_gather(own, "z", axis=0, tiled=True)
    (partial,) = kernel_call(
        cross_kernel, [((ZR, 2 * W), BF16)], [SM, VM, VM, VM], flops=1 << 29, moved=1 << 20
    )(pole_weights, block, columns, diag_inverse)
    both = lax.all_gather(partial, "c")
    density, quad = kernel_call(pair_kernel, [((ZR, W), BF16), ((NZ, W // NZ, W), BF16)], [VM], moved=1 << 19)(both)
    quad = lax.all_to_all(quad, "z", 0, 0)
    placed, *slabs = kernel_call(
        place_kernel,
        [((NX * NY, 4, 2 * W), BF16)] + [((W, HELD), BF16)] * HOLD,
        [VM, VM, pl.BlockSpec(memory_space=pl.ANY)],
        flops=1 << 23,
        moved=1 << 21,
        scratch=[pltpu.SemaphoreType.DMA((HOLD,))],
    )(block[:, 3 * RD :, :128], density, ham_slab)
    (joined,) = kernel_call(join_kernel, [((NX * NY, 4, 2 * W + 128), BF16)], [VM, VM], moved=1 << 18)(quad, placed)
    joined = lax.all_to_all(joined, ("x", "y"), 0, 0)
    streamed = NZ * NY * RD - HOLD * HELD
    density_diag, patch_energy = kernel_call(
        total_kernel,
        [((2, W), F32), ((CAP, NZ * NY * RD), BF16)],
        [VM] * (1 + HOLD) + [pl.BlockSpec(memory_space=pl.ANY)],
        flops=1 << 24,
        moved=1 << 18,
        kept=(False, False),
        scratch=[pltpu.VMEM((W, streamed), BF16), pltpu.SemaphoreType.DMA((streamed // PIECE,))],
    )(joined, *slabs, ham_slab)
    return (density_diag, patch_energy)


def solution(mesh):
    fine = Mesh(mesh.devices.reshape(NX, NC, NZ, NY), ("x", "c", "z", "y"))
    pole, grid = ("x", "c"), ("z", "y")
    by_row = P(pole, None, grid, None)
    return jax.shard_map(
        per_device,
        mesh=fine,
        in_specs=(by_row, by_row, by_row, P(pole, None), P(grid, None), P()),
        out_specs=(P(grid, None), P(("x", "c", "z", "y"), None)),
        check_vma=False,
    )
```

```python
import jax
import jax.numpy as jnp
from jax import lax
from jax.experimental import pallas as pl
from jax.experimental.pallas import tpu as pltpu
from jax.sharding import Mesh, PartitionSpec as P

NX, NC, NZ, NY = 4, 2, 16, 8
RD = 32
W = 256
ZR = NY * RD
YC = NZ * RD
CAP = 8
TAIL = 16
HOLD = 1
HELD = 3072
F32 = jnp.float32
BF16 = jnp.bfloat16
VM = pl.BlockSpec(memory_space=pltpu.VMEM)
SM = pl.BlockSpec(memory_space=pltpu.SMEM)


def kernel_call(body, outs, specs, flops=0, moved=0, kept=(True,) * 8, scratch=()):
    call = pl.pallas_call(
        body,
        out_shape=tuple(pltpu.VMEM(s, d) if k else jax.ShapeDtypeStruct(s, d) for (s, d), k in zip(outs, kept)),
        in_specs=specs,
        out_specs=tuple(VM for _ in outs),
        scratch_shapes=scratch,
        cost_estimate=pl.CostEstimate(flops=flops, bytes_accessed=moved, transcendentals=0),
    )

    def run(*args):
        return call(
            *(
                pltpu.with_memory_space_constraint(arg, pltpu.VMEM) if spec is VM else arg
                for arg, spec in zip(args, specs, strict=True)
            )
        )

    return run


def pack_kernel(o_hbm, g_hbm, l_hbm, out_hbm, own_ref, o_ref, g_ref, l_ref, out_ref, in_sem, out_sem):
    owners_in = pltpu.make_async_copy(o_hbm, o_ref, in_sem.at[0])
    rows_in = pltpu.make_async_copy(l_hbm, l_ref, in_sem.at[1])
    wide = NZ * W // 2
    pieces_in = [
        [
            pltpu.make_async_copy(
                g_hbm.at[0, part, :, pl.ds(wide * side, wide)],
                g_ref.at[part, :, pl.ds(wide * side, wide)],
                in_sem.at[2 + 2 * part + side],
            )
            for side in range(2)
        ]
        for part in range(2)
    ]
    spans = [(RD * part, RD, 256 * side, 256) for part in range(2) for side in range(2)] + [(2 * RD, RD + TAIL, 0, YC)]
    pieces_out = [
        pltpu.make_async_copy(
            out_ref.at[:, pl.ds(row, rows), pl.ds(lane, lanes)],
            out_hbm.at[:, pl.ds(row, rows), pl.ds(lane, lanes)],
            out_sem.at[i],
        )
        for i, (row, rows, lane, lanes) in enumerate(spans)
    ]
    owners_in.start()
    rows_in.start()
    for part in range(2):
        for side in range(2):
            pieces_in[part][side].start()
    rows_in.wait()
    for side in range(2):
        rows = l_ref[0, side]
        own_ref[0, :, W * side : W * side + W] = rows
        for y in range(NY):
            out_ref[y, 2 * RD : 3 * RD, W * side : W * side + W] = rows
    owners_in.wait()
    owner = jnp.broadcast_to(o_ref[...], (RD, RD))
    row = lax.broadcasted_iota(jnp.int32, (RD, RD), 0)
    column = lax.broadcasted_iota(jnp.int32, (RD, RD), 1)
    owner_down = jnp.sum(jnp.where(row == column, owner, 0), axis=1, keepdims=True)
    earlier = (owner_down == owner) & (row < column)
    rank = jnp.sum(earlier.astype(jnp.int32), axis=0, keepdims=True)
    slot = (o_ref[...] * CAP + rank).astype(F32)
    slot = jnp.broadcast_to(slot, (TAIL, RD)).astype(BF16)
    for y in range(NY):
        out_ref[y, 3 * RD :, :] = jnp.zeros((TAIL, YC), BF16)
        out_ref[y, 3 * RD :, 0:RD] = slot
    pieces_out[4].start()
    quarter = lax.broadcasted_iota(jnp.int32, (RD, 128), 1) // 32
    for part in range(2):
        for tile in range(4):
            if tile % 2 == 0:
                pieces_in[part][tile // 2].wait()
            for half in range(2):
                loaded = [
                    g_ref[part, :, (4 * tile + j) * W + half * 128 : (4 * tile + j) * W + half * 128 + 128].astype(F32)
                    for j in range(4)
                ]
                for q in range(4):
                    joined = None
                    for j in range(4):
                        shift = (32 * (j - q)) % 128
                        moved = pltpu.roll(loaded[j], shift, 1) if shift else loaded[j]
                        joined = moved if joined is None else jnp.where(quarter == j, moved, joined)
                    out_ref[4 * half + q, RD * part : RD * part + RD, 128 * tile : 128 * tile + 128] = joined.astype(BF16)
            if tile % 2 == 1:
                pieces_out[2 * part + tile // 2].start()
    for piece in pieces_out:
        piece.wait()


def pack(owner_map, trailing, panel):
    packed = (NY, 3 * RD + TAIL, YC)
    anywhere = pl.BlockSpec(memory_space=pl.ANY)
    return pl.pallas_call(
        pack_kernel,
        out_shape=(jax.ShapeDtypeStruct(packed, BF16), pltpu.VMEM((1, RD, 2 * W), BF16)),
        in_specs=[anywhere] * 3,
        out_specs=(anywhere, VM),
        scratch_shapes=[
            pltpu.VMEM((1, RD), jnp.int32),
            pltpu.VMEM((2, RD, NZ * W), BF16),
            pltpu.VMEM((1, 2, RD, W), BF16),
            pltpu.VMEM(packed, BF16),
            pltpu.SemaphoreType.DMA((6,)),
            pltpu.SemaphoreType.DMA((5,)),
        ],
        name="pack",
        cost_estimate=pl.CostEstimate(flops=0, bytes_accessed=1 << 20, transcendentals=0),
    )(owner_map.reshape(1, RD), trailing, panel)


def cross_kernel(w_ref, b_ref, l_ref, d_ref, out_ref):
    wr = w_ref[0, 0]
    wi = w_ref[0, 1]
    columns = l_ref[...].reshape(YC, 2 * W)
    first = jnp.dot(b_ref[:, 0:RD, :].reshape(ZR, YC), columns, preferred_element_type=F32)
    second = jnp.dot(b_ref[:, RD : 2 * RD, :].reshape(ZR, YC), columns, preferred_element_type=F32)
    real = first[:, :W] - second[:, W:]
    imag = first[:, W:] + second[:, :W]
    even = wr * imag + wi * real
    odd = wr * real - wi * imag
    rows = b_ref[:, 2 * RD : 3 * RD, :].reshape(ZR, 2 * W)
    over_rows = (((0,), (0,)), ((), ()))
    quad = lax.dot_general(rows[:, :W], even.astype(BF16), over_rows, preferred_element_type=F32)
    quad = quad + lax.dot_general(rows[:, W:], odd.astype(BF16), over_rows, preferred_element_type=F32)
    diag = wr * d_ref[0, 1].astype(F32) + wi * d_ref[0, 0].astype(F32)
    at = lax.axis_index("z") * (2 * NY) + lax.axis_index("y") * 2
    line = lax.broadcasted_iota(jnp.int32, (W, W), 0)
    for row in range(2):
        quad = quad + jnp.where(line == at + row, diag[row : row + 1], 0.0)
    out_ref[:, 0:W] = (-even).astype(BF16)
    out_ref[:, W:] = quad.astype(BF16)


def pair_kernel(p_ref, density_ref, quad_ref):
    quad_ref[...] = (p_ref[0, :, W:].astype(F32) + p_ref[1, :, W:].astype(F32)).astype(BF16).reshape(NZ, W // NZ, W)
    density_ref[...] = (p_ref[0, :, 0:W].astype(F32) + p_ref[1, :, 0:W].astype(F32)).astype(BF16)


def place_kernel(s_ref, d_ref, h_hbm, out_ref, *rest):
    slabs, sem = rest[:-1], rest[-1]
    pieces = [
        pltpu.make_async_copy(h_hbm.at[:, pl.ds(HELD * i, HELD)], slab, sem.at[i]) for i, slab in enumerate(slabs)
    ]
    for piece in pieces:
        piece.start()
    line = lax.broadcasted_iota(jnp.int32, (NX * CAP, RD), 0)
    index = (line // CAP * NC + lax.axis_index("c")) * CAP + line % CAP
    rows = d_ref[...]
    for y in range(NY):
        slot = s_ref[y, 0:1, 0:RD].astype(F32).astype(jnp.int32)
        place = (index == slot).astype(F32).astype(BF16)
        placed = jnp.dot(place, rows[RD * y : RD * y + RD], preferred_element_type=F32).astype(BF16)
        for x in range(NX):
            for part in range(2):
                start = CAP * x + 4 * part
                out_ref[NY * x + y, :, W * part : W * part + W] = placed[start : start + 4]
    for piece in pieces:
        piece.wait()


def join_kernel(q_ref, p_ref, out_ref):
    quad = jnp.sum(q_ref[...].astype(F32), axis=0)
    out_ref[:, :, 0 : 2 * W] = p_ref[...]
    for y in range(NY):
        rows = quad[2 * y : 2 * y + 2]
        tail = jnp.concatenate([rows[:, :128], rows[:, 128:]], axis=0).astype(BF16)
        for x in range(NX):
            out_ref[NY * x + y, :, 2 * W :] = tail


def total_kernel(p_ref, h_ref, h_hbm, diag_ref, energy_hbm, rest_ref, energy_ref, in_sem, out_sem):
    width = NZ * NY * RD
    rest_in = pltpu.make_async_copy(h_hbm.at[:, pl.ds(HELD, width - HELD)], rest_ref, in_sem)
    rest_in.start()
    total = jnp.sum(p_ref[...].astype(F32), axis=0)
    half = jnp.concatenate([total[:, :W], total[:, W : 2 * W]], axis=0).astype(BF16)
    spans = ((0, HELD), (HELD, width - HELD))
    pieces = [
        pltpu.make_async_copy(energy_ref.at[:, pl.ds(*span)], energy_hbm.at[:, pl.ds(*span)], out_sem.at[i])
        for i, span in enumerate(spans)
    ]
    energy_ref[:, 0:HELD] = jnp.dot(half, h_ref[...], preferred_element_type=F32).astype(BF16)
    pieces[0].start()
    rest_in.wait()
    energy_ref[:, HELD:] = jnp.dot(half, rest_ref[...], preferred_element_type=F32).astype(BF16)
    pieces[1].start()
    diag_ref[:, 0:128] = total[0:2, 2 * W :]
    diag_ref[:, 128:] = total[2:4, 2 * W :]
    for piece in pieces:
        piece.wait()


def energies(joined, slab, ham_slab):
    width = NZ * NY * RD
    anywhere = pl.BlockSpec(memory_space=pl.ANY)
    joined, slab = (pltpu.with_memory_space_constraint(value, pltpu.VMEM) for value in (joined, slab))
    return pl.pallas_call(
        total_kernel,
        out_shape=(jax.ShapeDtypeStruct((2, W), F32), jax.ShapeDtypeStruct((CAP, width), BF16)),
        in_specs=[VM, VM, anywhere],
        out_specs=(VM, anywhere),
        scratch_shapes=[
            pltpu.VMEM((W, width - HELD), BF16),
            pltpu.VMEM((CAP, width), BF16),
            pltpu.SemaphoreType.DMA,
            pltpu.SemaphoreType.DMA((2,)),
        ],
        name="total",
        cost_estimate=pl.CostEstimate(flops=1 << 24, bytes_accessed=1 << 18, transcendentals=0),
    )(joined, slab, ham_slab)


def per_device(trailing, panel, diag_inverse, pole_weights, owner_map, ham_slab):
    packed, own = pack(owner_map, trailing, panel)
    block = lax.all_to_all(packed, "y", 0, 0)
    columns = lax.all_gather(own, "z", axis=0, tiled=True)
    (partial,) = kernel_call(
        cross_kernel, [((ZR, 2 * W), BF16)], [SM, VM, VM, VM], flops=1 << 29, moved=1 << 20
    )(pole_weights, block, columns, diag_inverse)
    both = lax.all_gather(partial, "c")
    density, quad = kernel_call(pair_kernel, [((ZR, W), BF16), ((NZ, W // NZ, W), BF16)], [VM], moved=1 << 19)(both)
    quad = lax.all_to_all(quad, "z", 0, 0)
    placed, *slabs = kernel_call(
        place_kernel,
        [((NX * NY, 4, 2 * W), BF16)] + [((W, HELD), BF16)] * HOLD,
        [VM, VM, pl.BlockSpec(memory_space=pl.ANY)],
        flops=1 << 23,
        moved=1 << 21,
        scratch=[pltpu.SemaphoreType.DMA((HOLD,))],
    )(block[:, 3 * RD :, :128], density, ham_slab)
    (joined,) = kernel_call(join_kernel, [((NX * NY, 4, 2 * W + 128), BF16)], [VM, VM], moved=1 << 18)(quad, placed)
    joined = lax.all_to_all(joined, ("x", "y"), 0, 0)
    density_diag, patch_energy = energies(joined, slabs[0], ham_slab)
    return (density_diag, patch_energy)


def solution(mesh):
    fine = Mesh(mesh.devices.reshape(NX, NC, NZ, NY), ("x", "c", "z", "y"))
    pole, grid = ("x", "c"), ("z", "y")
    by_row = P(pole, None, grid, None)
    return jax.shard_map(
        per_device,
        mesh=fine,
        in_specs=(by_row, by_row, by_row, P(pole, None), P(grid, None), P()),
        out_specs=(P(grid, None), P(("x", "c", "z", "y"), None)),
        check_vma=False,
    )
```
